32 devices in a mesh: chain: 16 (over z, y, core), aux: 2 (over x).
Axes of the slice: x: 2, y: 2, z: 4, core: 2. Of those that a mesh axis runs over, the one named last changes fastest.
Arguments:
- occupied: bfloat16 [2048, 1152], P('chain'), may hold values from -0.1875 to 0.1875
- virtual: bfloat16 [2048, 1152], P('chain'), may hold values from -0.1875 to 0.1875
- three_centre: bfloat16 [32, 2048, 1152], P('aux', 'chain'), may hold values from -6 to 6
- kernel: bfloat16 [32, 32], P('aux'), may hold values from -1 to 1
- profile: int32 [16], replicated, may hold values from 2 to 4
- atom_map: int32 [32], P('aux'), may hold values from 0 to 15
Outputs:
- band_gradient: float32 [2048, 1152], P(('chain', 'aux'))
- polarization: float32 [32, 32], P('aux')
The draws below stay inside these ranges and needn't reach their ends.
All inputs are finite; a program needn't handle non-finite values.
Results may differ from the reference program's by a relative error of at most 0.0042.
Values may be sent and summed in bfloat16 or wider, within the bound.
No kernel may reach another device: no remote copies, remote signals or barrier semaphores. Data moves between devices by JAX's collectives and lax.ppermute only.
A program may use at most 128 MiB of HBM per device.

```python
import math
import jax
import jax.numpy as jnp
from jax import lax

BLOCK = 128
BAND = 4
NBLK = 16
NBAS = 2048
NAUX = 32
BANDW = 1152
REACH = 4


def with_ends(values, stream_key, smallest, largest):
    extent = values.shape
    index_at = [jax.random.randint(jax.random.fold_in(stream_key, axis), (), 0, extent[axis]) for axis in range(len(extent))]
    values = values.at[tuple(index_at)].set(smallest)
    longest = extent.index(max(extent))
    index_at[longest] = (index_at[longest] + 1) % extent[longest]
    return values.at[tuple(index_at)].set(largest)


def levels(own_key, shape, split, smallest, top_value):
    level = 1.0
    for axis_at, shards_of in split:
        heights = jax.random.uniform(jax.random.fold_in(jax.random.fold_in(own_key, 6), axis_at), (shards_of,), jnp.float32, smallest / len(split), top_value / len(split))
        level = level * jnp.repeat(jnp.exp(heights), shape[axis_at] // shards_of).reshape((-1,) + (1,) * (len(shape) - 1 - axis_at))
    return level


def gaussian(key, shape, spread, bound, split=(), held_as=jnp.bfloat16):
    gain = levels(key, shape, split, -0.22, 0.18) if split else 1.0
    result = jax.random.normal(key, shape, jnp.float32) * spread * gain
    return jnp.minimum(jnp.maximum(result, -bound), bound).astype(held_as)


def setup_inputs(seed: int = 0) -> dict:
    keys = jax.random.split(jax.random.key(seed), 7)
    return {
        "occupied": gaussian(keys[0], (NBAS, BANDW), BANDW ** -0.5, 0.1875, ((0, 16),)),
        "virtual": gaussian(keys[1], (NBAS, BANDW), BANDW ** -0.5, 0.1875, ((0, 16),)),
        "three_centre": gaussian(keys[2], (NAUX, NBAS, BANDW), 1.0, 6.0, ((0, 2), (1, 16))),
        "kernel": gaussian(keys[3], (NAUX, NAUX), NAUX ** -0.5, 1.0, ((0, 2),)),
        "profile": with_ends(jax.random.randint(keys[4], (NBLK,), 2, BAND + 1), jax.random.fold_in(keys[4], 1), 2, BAND).astype(jnp.int32),
        "atom_map": with_ends(jax.random.randint(keys[5], (NAUX,), 0, NBLK), jax.random.fold_in(keys[5], 1), 0, NBLK - 1).astype(jnp.int32),
    }


def shift_blocks(matrix, offset, block_size):
    if offset == 0:
        return matrix
    padding = jnp.zeros(matrix.shape[:-1] + (abs(offset) * block_size,), matrix.dtype)
    if offset > 0:
        return jnp.concatenate([padding, matrix[..., :-offset * block_size]], -1)
    return jnp.concatenate([matrix[..., -offset * block_size:], padding], -1)

def reference(occupied, virtual, three_centre, kernel, profile, atom_map):
    slots_total = 2 * BAND + 1
    indices = jnp.arange(NBLK, dtype=jnp.int32)
    padded_profile = jnp.pad(profile, BAND)
    neighbours = jnp.stack([padded_profile[slot_index:slot_index + NBLK] for slot_index in range(slots_total)], 1)
    distance = jnp.abs(jnp.arange(slots_total, dtype=jnp.int32) - BAND)
    allowed = distance[None, :] <= jnp.minimum(profile[:, None], neighbours)
    column_mask = jnp.repeat(allowed, BLOCK, axis=1)
    zero_half = jnp.zeros((), jnp.bfloat16)
    occ_rows = jnp.where(column_mask[:, None, :], occupied.reshape(NBLK, BLOCK, BANDW), zero_half)
    vir_rows = jnp.where(column_mask[:, None, :], virtual.reshape(NBLK, BLOCK, BANDW), zero_half)
    occ_padded = jnp.pad(occ_rows, ((BAND, BAND), (0, 0), (0, 0)))
    vir_padded = jnp.pad(vir_rows, ((BAND, BAND), (0, 0), (0, 0)))
    integrals = three_centre.reshape(NAUX, NBLK, BLOCK, BANDW)
    screen = jnp.abs(atom_map[:, None] - indices[None, :]) <= REACH

    def per_block(state_pair, block_index):
        gradient_pad, polar_sum = state_pair
        near_occ = lax.dynamic_slice_in_dim(occ_padded, block_index, slots_total, 0)
        near_vir = lax.dynamic_slice_in_dim(vir_padded, block_index, slots_total, 0)
        stack_occ = jnp.concatenate([shift_blocks(near_occ[k], k - BAND, BLOCK) for k in range(slots_total)], 0)
        stack_vir = jnp.concatenate([shift_blocks(near_vir[k], k - BAND, BLOCK) for k in range(slots_total)], 0)
        local = lax.dynamic_index_in_dim(integrals, block_index, 1, keepdims=False)
        col_keep = lax.dynamic_index_in_dim(column_mask, block_index, 0, keepdims=False)
        aux_keep = lax.dynamic_index_in_dim(screen, block_index, 1, keepdims=False)
        local = jnp.where(col_keep[None, None, :] & aux_keep[:, None, None], local, zero_half)
        screened = local.reshape(NAUX * BLOCK, BANDW)
        coupled = jnp.dot(screened, stack_occ, preferred_element_type=jnp.float32).astype(jnp.bfloat16)
        partner = jnp.dot(screened, stack_vir, preferred_element_type=jnp.float32).astype(jnp.bfloat16)
        coupled_rows = coupled.reshape(NAUX, BLOCK * BANDW)
        partner_rows = partner.reshape(NAUX, BLOCK * BANDW)
        polar_sum = polar_sum + jnp.dot(coupled_rows, partner_rows.T, preferred_element_type=jnp.float32)
        response = jnp.dot(kernel, partner_rows, preferred_element_type=jnp.float32).astype(jnp.bfloat16)
        partials = lax.dot_general(screened, response.reshape(NAUX * BLOCK, BANDW), (((0,), (0,)), ((), ())), preferred_element_type=jnp.float32)
        partials = partials.reshape(slots_total, BLOCK, BANDW)
        moved = jnp.stack([shift_blocks(partials[k], BAND - k, BLOCK) for k in range(slots_total)], 0)
        current = lax.dynamic_slice_in_dim(gradient_pad, block_index, slots_total, 0)
        gradient_pad = lax.dynamic_update_slice_in_dim(gradient_pad, current + moved, block_index, 0)
        return ((gradient_pad, polar_sum), None)
    initial = (jnp.zeros((NBLK + 2 * BAND, BLOCK, BANDW), jnp.float32), jnp.zeros((NAUX, NAUX), jnp.float32))
    (gradient_pad, polar_sum), unused = lax.scan(per_block, initial, indices)
    scale_grad = 1.0 / math.sqrt(BLOCK * NAUX)
    scale_pol = 1.0 / math.sqrt(NBAS * BANDW)
    gradient = jnp.where(column_mask[:, None, :], gradient_pad[BAND:BAND + NBLK], jnp.zeros((), jnp.float32)) * scale_grad
    return (gradient.reshape(NBAS, BANDW), polar_sum * scale_pol)
```

```python
import functools
import math

import jax
import jax.numpy as jnp
from jax import lax
from jax.experimental import pallas as pl
from jax.experimental.pallas import tpu as pltpu
from jax.sharding import PartitionSpec as P

F32 = jnp.float32
BF16 = jnp.bfloat16
SUB = 8
CHUNKS = 4
VMEM = pl.BlockSpec(memory_space=pltpu.VMEM)
SMEM = pl.BlockSpec(memory_space=pltpu.SMEM)
PARAMS = pltpu.CompilerParams(vmem_limit_bytes=60 * 1024 * 1024)


def passed_along(block, axis, distance):
    devices = range(lax.axis_size(axis))
    route = [(i - distance, i) for i in devices if i - distance in devices]
    return lax.ppermute(block, axis, route)


def swapped(block, axis, bit=1):
    return lax.ppermute(block, axis, [(i, i ^ bit) for i in range(lax.axis_size(axis))])


def permitted(prof_ref, nblocks, a, b):
    last = nblocks - 1
    inside = (a >= 0) & (a <= last) & (b >= 0) & (b <= last)
    wide_a = prof_ref[jnp.clip(a, 0, last)]
    wide_b = prof_ref[jnp.clip(b, 0, last)]
    return inside & (jnp.abs(a - b) <= jnp.minimum(wide_a, wide_b))


def cost(flops, nbytes):
    return pl.CostEstimate(flops=int(flops), bytes_accessed=int(nbytes), transcendentals=0)


def stack_kernel(dims, at_ref, prof_ref, *refs):
    nblocks, block, slots = dims
    spread = (slots - 1) // 2
    width = slots * block
    same = dict(zip((-4, -2, 0, 2, 4), refs[:5]))
    near_low, near_mid, near_high, far_even, far_odd = refs[5:10]
    own_ref, xv_ref, cp_ref = refs[10:]
    position = at_ref[0]
    odd = lax.rem(position, 2) == 1

    def assemble(offset, source):
        rows = slice((offset + spread) * block, (offset + spread + 1) * block)
        other = position + offset
        row_ok = permitted(prof_ref, nblocks, position, other)
        for col in range(slots):
            slot = col - offset
            for half in range(2):
                columns = slice(half * width + col * block, half * width + (col + 1) * block)
                if 0 <= slot < slots:
                    ok = row_ok & permitted(prof_ref, nblocks, other, position + col - spread)
                    tile = source[half, :, slot * block : (slot + 1) * block]
                    xv_ref[rows, columns] = jnp.where(ok, tile, jnp.zeros_like(tile))
                else:
                    xv_ref[rows, columns] = jnp.zeros((block, block), BF16)

    for offset in (-4, -2, 0, 2, 4):
        assemble(offset, same[offset])

    @pl.when(jnp.logical_not(odd))
    def _():
        for offset, source in ((-3, far_odd), (-1, near_low), (1, near_mid), (3, near_high)):
            assemble(offset, source)

    @pl.when(odd)
    def _():
        for offset, source in ((-3, near_low), (-1, near_mid), (1, near_high), (3, far_even)):
            assemble(offset, source)

    contract(own_ref, xv_ref, cp_ref)


def contract(rows_ref, xv_ref, out_ref, tile=256):
    @pl.loop(0, xv_ref.shape[1] // tile)
    def _(n):
        columns = pl.ds(pl.multiple_of(n * tile, tile), tile)
        out_ref[:, columns] = jnp.dot(
            rows_ref[...], xv_ref[:, columns], preferred_element_type=F32
        ).astype(out_ref.dtype)


def one_hot(rows, cols):
    r = lax.broadcasted_iota(jnp.int32, (rows, cols), 0)
    c = lax.broadcasted_iota(jnp.int32, (rows, cols), 1)
    return (r // SUB == c).astype(F32)


def same_row(size):
    r = lax.broadcasted_iota(jnp.int32, (size, size), 0)
    c = lax.broadcasted_iota(jnp.int32, (size, size), 1)
    return lax.rem(r, SUB) == lax.rem(c, SUB)


def response_kernel(last, k_ref, s_ref, xv_ref, cp_ref, g_in, ro_ref, rr_ref, g_ref, cr_ref):
    width = xv_ref.shape[1] // 2
    size = k_ref.shape[0] * SUB
    half = size // 2
    contract(s_ref, xv_ref, cr_ref)
    pick = one_hot(size, k_ref.shape[0]).astype(BF16)
    spread_k = jnp.dot(pick, k_ref[...], preferred_element_type=F32).astype(BF16)
    spread_k = lax.dot_general(
        spread_k, pick, (((1,), (1,)), ((), ())), preferred_element_type=F32
    )
    diag = same_row(size)
    mixed = jnp.where(diag, spread_k, 0.0).astype(BF16)
    total = g_in[...]
    for g in range(s_ref.shape[0] // half):
        rows = slice(g * half, (g + 1) * half)
        coupled = jnp.concatenate([cp_ref[rows, :width], cr_ref[rows, :width]], 0)
        partner = jnp.concatenate([cp_ref[rows, width:], cr_ref[rows, width:]], 0)
        total = total + lax.dot_general(
            coupled, partner, (((1,), (1,)), ((), ())), preferred_element_type=F32
        )
        resp = jnp.dot(mixed, partner, preferred_element_type=F32).astype(BF16)
        ro_ref[rows, :] = resp[:half]
        rr_ref[rows, :] = resp[half:]
    if last:
        count = k_ref.shape[0]
        by_row = jnp.sum(jnp.where(diag, total, 0.0).reshape(count, SUB, size), 1)
        g_ref[...] = jnp.dot(
            by_row, one_hot(size, count), preferred_element_type=F32, precision=lax.Precision.HIGHEST
        )
    else:
        g_ref[...] = total


def add_terms(pairs, first, columns, acc):
    for s_ref, r_ref in pairs:
        part = lax.dot_general(
            s_ref[...], r_ref[:, columns], (((0,), (0,)), ((), ())), preferred_element_type=F32
        )
        acc = part if acc is None else acc + part
    return acc


def early_terms_kernel(count, *refs):
    ins, out_ref = refs[: 2 * count], refs[2 * count]
    pairs = list(zip(ins[:count], ins[count:]))
    tile = 384

    @pl.loop(0, out_ref.shape[1] // tile)
    def _(n):
        columns = pl.ds(pl.multiple_of(n * tile, tile), tile)
        out_ref[:, columns] = add_terms(pairs, True, columns, None)


def late_terms_kernel(dims, count, at_ref, prof_ref, early_ref, *refs):
    nblocks, block, slots = dims
    spread = (slots - 1) // 2
    ins, outs = refs[: 2 * count], refs[2 * count :]
    pairs = list(zip(ins[:count], ins[count:]))
    position = at_ref[0]
    tile = 3 * block
    for n in range(slots * block // tile):
        columns = slice(n * tile, (n + 1) * tile)
        total = add_terms(pairs, False, columns, early_ref[:, columns])
        for k in range(slots):
            offset = k - spread
            ok = permitted(prof_ref, nblocks, position, position + offset)
            part = total[k * block : (k + 1) * block]
            part = jnp.where(ok, part, jnp.zeros_like(part)).astype(outs[k].dtype)
            for c in range(3):
                at = n * 3 + c - max(0, offset)
                if 0 <= at < slots - abs(offset):
                    outs[k][:, at * block : (at + 1) * block] = part[:, c * block : (c + 1) * block]


def sum_kernel(dims, at_ref, *refs):
    nblocks, block, slots = dims
    spread = (slots - 1) // 2
    parts, (keep_ref, send_ref) = refs[:slots], refs[slots:]
    rows = keep_ref.shape[0]
    half = at_ref[1]
    for target, first in ((keep_ref, half), (send_ref, 1 - half)):
        window = pl.ds(pl.multiple_of(first * rows, rows), rows)
        for c in range(slots):
            total = None
            for k in range(slots):
                offset = k - spread
                at = c - max(0, -offset)
                if 0 <= at < slots - abs(offset):
                    term = parts[k][window, at * block : (at + 1) * block].astype(F32)
                    total = term if total is None else total + term
            target[:, c * block : (c + 1) * block] = total.astype(target.dtype)


def finish_kernel(dims, scale, at_ref, prof_ref, keep_ref, got_ref, out_ref):
    nblocks, block, slots = dims
    spread = (slots - 1) // 2
    position = at_ref[0]
    for c in range(slots):
        columns = slice(c * block, (c + 1) * block)
        ok = permitted(prof_ref, nblocks, position, position + c - spread)
        value = (keep_ref[:, columns] + got_ref[:, columns].astype(F32)) * scale
        out_ref[:, columns] = jnp.where(ok, value, jnp.zeros_like(value))


def body(occupied, virtual, three_centre, kernel, profile, atom_map):
    block, width = occupied.shape
    slots = width // block
    spread = (slots - 1) // 2
    nblocks = lax.axis_size("chain")
    halves = lax.axis_size("aux")
    if halves != 2 or spread != 4 or nblocks % 2:
        raise ValueError("unsupported mesh")
    position = lax.axis_index("chain")
    half = lax.axis_index("aux")
    here = three_centre.shape[0]
    every = kernel.shape[1]
    dims = (nblocks, block, slots)
    rows = block // halves
    groups = rows // SUB
    per_group = here * SUB
    per_chunk = groups // CHUNKS
    at = jnp.stack([position, half]).astype(jnp.int32)

    def rows_of(which, first, count):
        start = which * rows + first * SUB
        part = lax.dynamic_slice(three_centre, (0, start, 0), (here, count * SUB, width))
        part = part.reshape(here, count, SUB, width).transpose(1, 0, 2, 3)
        return part.reshape(count * per_group, width)

    received = [
        swapped(rows_of(1 - half, c * per_chunk, per_chunk), "aux") for c in range(CHUNKS)
    ]

    pack = jnp.stack([occupied, virtual])
    same = {d: pack if d == 0 else passed_along(pack, "chain", -d) for d in (-4, -2, 0, 2, 4)}
    near = [swapped(same[d], "chain") for d in (-2, 0, 2)]
    far_even = lax.ppermute(same[4], "chain", [(i, i + 1) for i in range(0, nblocks, 2)])
    far_odd = lax.ppermute(same[-4], "chain", [(i + 1, i) for i in range(0, nblocks, 2)])

    active = (jnp.abs(atom_map - position) <= nblocks // 4).astype(F32)
    ordered = jnp.where(half == 0, kernel, jnp.roll(kernel, here, 1)).astype(F32)
    mine = jnp.concatenate([ordered * active[:, None], active[:, None]], 1)
    theirs = swapped(mine, "aux")
    theirs = jnp.concatenate([jnp.roll(theirs[:, :every], here, 1), theirs[:, every:]], 1)
    small = jnp.concatenate([mine, theirs], 0)
    alive = small[:, every]
    mixing = (small[:, :every] * alive[None, :]).astype(BF16)

    own = rows_of(half, 0, groups)
    own_rows = groups * per_group
    xv, cp = pl.pallas_call(
        functools.partial(stack_kernel, dims),
        out_shape=(
            jax.ShapeDtypeStruct((width, 2 * width), BF16),
            jax.ShapeDtypeStruct((own_rows, 2 * width), BF16),
        ),
        in_specs=[SMEM, SMEM] + [VMEM] * 11,
        out_specs=(VMEM, VMEM),
        compiler_params=PARAMS,
        cost_estimate=cost(4 * own_rows * width * width, 12 * own_rows * width),
        name="stack",
    )(at, profile, *[same[d] for d in (-4, -2, 0, 2, 4)], *near, far_even, far_odd, own)

    span = per_chunk * per_group
    gram = jnp.zeros((every * SUB, every * SUB), F32)
    pairs = []
    for c in range(CHUNKS):
        last = c == CHUNKS - 1
        gram_shape = (every, every) if last else (every * SUB, every * SUB)
        chunk_rows = slice(c * span, (c + 1) * span)
        r_own, r_got, gram = pl.pallas_call(
            functools.partial(response_kernel, last),
            out_shape=(
                jax.ShapeDtypeStruct((span, width), BF16),
                jax.ShapeDtypeStruct((span, width), BF16),
                jax.ShapeDtypeStruct(gram_shape, F32),
            ),
            in_specs=[VMEM] * 5,
            out_specs=(VMEM, VMEM, VMEM),
            scratch_shapes=[pltpu.VMEM((span, 2 * width), BF16)],
            compiler_params=PARAMS,
            cost_estimate=cost(4 * span * width * width, 12 * span * width),
            name="respond",
        )(mixing, received[c], xv, cp[chunk_rows], gram)
        pairs.append(((own[chunk_rows], r_own), (received[c], r_got)))

    early = [p for c in range(CHUNKS - 1) for p in pairs[c]]
    early_terms = pl.pallas_call(
        functools.partial(early_terms_kernel, len(early)),
        out_shape=jax.ShapeDtypeStruct((width, width), F32),
        in_specs=[VMEM] * (2 * len(early)),
        out_specs=VMEM,
        compiler_params=PARAMS,
        cost_estimate=cost(2 * len(early) * span * width * width, 4 * width * width),
        name="early",
    )(*[s for s, _ in early], *[r for _, r in early])
    late = pairs[-1]
    shapes = [
        jax.ShapeDtypeStruct((block, (slots - abs(k - spread)) * block), F32 if k == spread else BF16)
        for k in range(slots)
    ]
    parts = pl.pallas_call(
        functools.partial(late_terms_kernel, dims, len(late)),
        out_shape=shapes,
        in_specs=[SMEM, SMEM] + [VMEM] * (1 + 2 * len(late)),
        out_specs=[VMEM] * slots,
        compiler_params=PARAMS,
        cost_estimate=cost(4 * span * width * width, 6 * width * width),
        name="late",
    )(at, profile, early_terms, *[s for s, _ in late], *[r for _, r in late])

    arrived = [
        parts[k] if k == spread else passed_along(parts[k], "chain", k - spread)
        for k in range(slots)
    ]
    keep, send = pl.pallas_call(
        functools.partial(sum_kernel, dims),
        out_shape=(
            jax.ShapeDtypeStruct((rows, width), F32),
            jax.ShapeDtypeStruct((rows, width), BF16),
        ),
        in_specs=[SMEM] + [VMEM] * slots,
        out_specs=(VMEM, VMEM),
        compiler_params=PARAMS,
        name="gather_terms",
    )(at, *arrived)
    got = swapped(send, "aux")
    band_gradient = pl.pallas_call(
        functools.partial(finish_kernel, dims, 1.0 / math.sqrt(block * every)),
        out_shape=jax.ShapeDtypeStruct((rows, width), F32),
        in_specs=[SMEM, SMEM, VMEM, VMEM],
        out_specs=VMEM,
        compiler_params=PARAMS,
        name="finish",
    )(at, profile, keep, got)

    polar = gram * alive[:, None] * alive[None, :]
    theirs = swapped(polar[here:], "aux")
    polar = polar[:here] + jnp.roll(theirs, here, 1)
    bit = 1
    while bit < nblocks:
        polar = polar + swapped(polar, "chain", bit)
        bit *= 2
    polar = jnp.where(half == 0, polar, jnp.roll(polar, here, 1))
    polarization = polar * (1.0 / math.sqrt(block * nblocks * width))
    return (band_gradient, polarization)


def solution(mesh):
    placed = (
        P("chain", None),
        P("chain", None),
        P("aux", "chain", None),
        P("aux", None),
        P(),
        P("aux"),
    )
    return jax.shard_map(
        body,
        mesh=mesh,
        in_specs=placed,
        out_specs=(P(("chain", "aux"), None), P("aux", None)),
        check_vma=False,
    )
```

```python
import functools
import math

import jax
import jax.numpy as jnp
from jax import lax
from jax.experimental import pallas as pl
from jax.experimental.pallas import tpu as pltpu
from jax.sharding import PartitionSpec as P


F32 = jnp.float32
BF16 = jnp.bfloat16
SUB = 8
CHUNKS = 4
SPREAD = 4
SLOTS = 9
VMEM = pl.BlockSpec(memory_space=pltpu.VMEM)
SMEM = pl.BlockSpec(memory_space=pltpu.SMEM)
FIRST_COLUMN = {2: 0, -2: 1, 4: 0, -4: 3, 1: 0, 3: 0, -1: 1, -3: 1}
ODD = (-3, -1, 1, 3)


def columns_to(offset):
    return 6 if abs(offset) == 4 else 8


def passed_along(block, axis, distance):
    devices = range(lax.axis_size(axis))
    route = [(i - distance, i) for i in devices if i - distance in devices]
    return lax.ppermute(block, axis, route)


def swapped(block, axis, bit=1):
    return lax.ppermute(block, axis, [(i, i ^ bit) for i in range(lax.axis_size(axis))])


def permitted(prof_ref, nblocks, a, b):
    last = nblocks - 1
    inside = (a >= 0) & (a <= last) & (b >= 0) & (b <= last)
    wide_a = prof_ref[jnp.clip(a, 0, last)]
    wide_b = prof_ref[jnp.clip(b, 0, last)]
    return inside & (jnp.abs(a - b) <= jnp.minimum(wide_a, wide_b))


def run(kernel, operands, outs, flops=0, scratch=(), smem=0, grant=24):
    nbytes = sum(math.prod(s.shape) * s.dtype.itemsize for s in (*operands, *outs))
    return pl.pallas_call(
        kernel,
        out_shape=outs,
        in_specs=[SMEM] * smem + [VMEM] * (len(operands) - smem),
        out_specs=[VMEM] * len(outs),
        scratch_shapes=list(scratch),
        compiler_params=pltpu.CompilerParams(vmem_limit_bytes=grant * 1024 * 1024),
        cost_estimate=pl.CostEstimate(
            flops=int(flops), bytes_accessed=int(nbytes), transcendentals=0
        ),
    )(*operands)


def shaped(shape, dtype=BF16):
    return jax.ShapeDtypeStruct(shape, dtype)


def dot(a, b):
    return jnp.dot(a, b, preferred_element_type=F32)


def dot_rows(a, b):
    return lax.dot_general(a, b, (((0,), (0,)), ((), ())), preferred_element_type=F32)


def dot_columns(a, b):
    return lax.dot_general(a, b, (((1,), (1,)), ((), ())), preferred_element_type=F32)


def prepare_kernel(nblocks, at_ref, atom_ref, k_ref, keep_ref, send_ref):
    here, every = k_ref.shape
    position, half = at_ref[0], at_ref[1]
    rows = lax.broadcasted_iota(jnp.int32, (here, every), 0)
    alive = jnp.zeros((here, every), F32)
    for p in range(here):
        near = jnp.abs(atom_ref[p] - position) <= nblocks // 4
        alive = jnp.where((rows == p) & near, 1.0, alive)
    plain = k_ref[...].astype(F32) * alive
    turned = jnp.concatenate([plain[:, here:], plain[:, :here]], 1)
    keep_ref[:, :every] = jnp.where(half == 0, plain, turned)
    keep_ref[:, every:] = alive
    send_ref[:, :every] = jnp.where(half == 0, turned, plain)
    send_ref[:, every:] = alive


def screen_row(mine_ref, theirs_ref):
    every = mine_ref.shape[1] // 2
    alive = jnp.concatenate([mine_ref[:, every:], theirs_ref[:, every:]], 0)
    r = lax.broadcasted_iota(jnp.int32, (every, every), 0)
    c = lax.broadcasted_iota(jnp.int32, (every, every), 1)
    return jnp.sum(jnp.where(r == c, alive, 0.0), 0, keepdims=True), alive


def one_hot(rows, cols):
    r = lax.broadcasted_iota(jnp.int32, (rows, cols), 0)
    c = lax.broadcasted_iota(jnp.int32, (rows, cols), 1)
    return (r // SUB == c).astype(F32)


def same_row(size):
    r = lax.broadcasted_iota(jnp.int32, (size, size), 0)
    c = lax.broadcasted_iota(jnp.int32, (size, size), 1)
    return lax.rem(r, SUB) == lax.rem(c, SUB)


def mixing_matrix(mine_ref, theirs_ref):
    every = mine_ref.shape[1] // 2
    size = every * SUB
    row, _ = screen_row(mine_ref, theirs_ref)
    k = jnp.concatenate([mine_ref[:, :every], theirs_ref[:, :every]], 0) * row
    pick = one_hot(size, every).astype(BF16)
    wide = dot_columns(dot(pick, k.astype(BF16)).astype(BF16), pick)
    return jnp.where(same_row(size), wide, 0.0).astype(BF16)


def band_slots(delta, which):
    sizes = {1: (7, 8), 2: (5, 6), -1: (8, 7), -2: (6, 5)}[delta]
    count = sizes[which]
    first = SLOTS - count if delta > 0 else 0
    return first, count, sizes[0] * which


def pair_kernel(at_ref, own_ref, mid_ref, out1_ref, out2_ref):
    block = own_ref.shape[0]

    def fill(sign, pair):
        for distance, out in ((1, out1_ref), (2, out2_ref)):
            for which in range(2):
                first, count, start = band_slots(sign * distance, which)
                out[:, start * block : (start + count) * block] = pair[which][
                    :, first * block : (first + count) * block
                ]

    odd = lax.rem(at_ref[0], 2) == 1

    @pl.when(jnp.logical_not(odd))
    def _():
        fill(1, (own_ref, mid_ref))

    @pl.when(odd)
    def _():
        fill(-1, (mid_ref, own_ref))


def stack_kernel(nblocks, counts, at_ref, prof_ref, *refs):
    own_ref, mid_ref, hop1_ref, hop2_ref, near1_ref, near2_ref = refs[:6]
    owns = refs[6 : 6 + counts]
    stack_ref, outs = refs[6 + counts], refs[7 + counts :]
    block = own_ref.shape[0]
    position = at_ref[0]

    def build(parity, pair, below, above):
        for offset in range(-SPREAD, SPREAD + 1):
            delta, which = divmod(parity + offset, 2)
            rows = slice((offset + SPREAD) * block, (offset + SPREAD + 1) * block)
            other = position + offset
            row_ok = permitted(prof_ref, nblocks, position, other)
            for col in range(SLOTS):
                slot = col - offset
                columns = slice(col * block, (col + 1) * block)
                if not 0 <= slot < SLOTS:
                    stack_ref[rows, columns] = jnp.zeros((block, block), BF16)
                    continue
                if delta == 0:
                    source, at = pair[which], slot
                else:
                    first, _, start = band_slots(-delta, which)
                    source = (below if delta < 0 else above)[abs(delta) - 1]
                    at = start + slot - first
                ok = row_ok & permitted(prof_ref, nblocks, other, position + col - SPREAD)
                tile = source[:, at * block : (at + 1) * block]
                stack_ref[rows, columns] = jnp.where(ok, tile, jnp.zeros_like(tile))

    odd = lax.rem(position, 2) == 1
    hops, nears = (hop1_ref, hop2_ref), (near1_ref, near2_ref)

    @pl.when(jnp.logical_not(odd))
    def _():
        build(0, (own_ref, mid_ref), hops, nears)

    @pl.when(odd)
    def _():
        build(1, (mid_ref, own_ref), nears, hops)

    for own, out in zip(owns, outs):
        out[...] = dot(own[...], stack_ref[...]).astype(BF16)


def cut_kernel(rows, picks, at_ref, three_ref, *refs):
    outs, sem = refs[:-1], refs[-1]
    copies = []
    for (mine, first), out in zip(picks, outs):
        which = at_ref[1] if mine else 1 - at_ref[1]
        for g in range(out.shape[0]):
            start = pl.multiple_of(which * rows + (first + g) * SUB, SUB)
            copies.append(
                pltpu.make_async_copy(
                    three_ref.at[:, pl.ds(start, SUB), :], out.at[g], sem.at[len(copies)]
                )
            )
    for copy in copies:
        copy.start()
    for copy in copies:
        copy.wait()


def respond(mixed, po_ref, pr_ref, ro_ref, rr_ref):
    half = mixed.shape[0] // 2
    for g in range(po_ref.shape[0] // half):
        rows = slice(g * half, (g + 1) * half)
        partner = jnp.concatenate([po_ref[rows, :], pr_ref[rows, :]], 0)
        resp = dot(mixed, partner).astype(BF16)
        ro_ref[rows, :] = resp[:half]
        rr_ref[rows, :] = resp[half:]


def respond_kernel(mine_ref, theirs_ref, v_ref, s_ref, po_ref, pr_ref, ro_ref, rr_ref):
    pr_ref[...] = dot(s_ref[...], v_ref[...]).astype(BF16)
    respond(mixing_matrix(mine_ref, theirs_ref), po_ref, pr_ref, ro_ref, rr_ref)


def early_kernel(count, *refs):
    out_ref = refs[2 * count]
    for c in range(0, out_ref.shape[1], 384):
        columns = slice(c, c + 384)
        acc = None
        for s_ref, r_ref in zip(refs[:count], refs[count : 2 * count]):
            part = dot_rows(s_ref[...], r_ref[:, columns])
            acc = part if acc is None else acc + part
        out_ref[:, columns] = acc


def terms_of(offsets, early_ref, so_ref, sr_ref, ro_ref, rr_ref, block):
    take = [slice((d + SPREAD) * block, (d + SPREAD + 1) * block) for d in offsets]
    own = jnp.concatenate([so_ref[:, t] for t in take], 1)
    got = jnp.concatenate([sr_ref[:, t] for t in take], 1)
    total = dot_rows(own, ro_ref[...]) + dot_rows(got, rr_ref[...])
    return [total[n * block : (n + 1) * block] + early_ref[t, :] for n, t in enumerate(take)]


def placed_terms(ok, term, offset, first, count, block, dtype):
    tiles = []
    for c in range(first, first + count):
        source = c + offset
        if 0 <= source < SLOTS:
            tile = term[:, source * block : (source + 1) * block]
            tiles.append(jnp.where(ok, tile, jnp.zeros_like(tile)).astype(dtype))
        else:
            tiles.append(jnp.zeros((block, block), dtype))
    return tiles


def odd_kernel(
    nblocks, at_ref, prof_ref, mine_ref, theirs_ref, v_ref, s_ref, po_ref, so_ref, early_ref,
    pr_ref, ro_ref, rr_ref, pack_ref,
):
    respond_kernel(mine_ref, theirs_ref, v_ref, s_ref, po_ref, pr_ref, ro_ref, rr_ref)
    block = pack_ref.shape[1]
    position = at_ref[0]
    terms = terms_of(ODD, early_ref, so_ref, s_ref, ro_ref, rr_ref, block)
    for n, (offset, term) in enumerate(zip(ODD, terms)):
        ok = permitted(prof_ref, nblocks, position, position + offset)
        tiles = placed_terms(ok, term, offset, FIRST_COLUMN[offset], 8, block, BF16)
        for c, tile in enumerate(tiles):
            pack_ref[n, :, c * block : (c + 1) * block] = tile


def even_kernel(
    nblocks, at_ref, prof_ref, so_ref, s_ref, ro_ref, rr_ref, early_ref, own_ref, *out_refs
):
    block = own_ref.shape[0]
    position = at_ref[0]
    offsets = (0, 2, -2, 4, -4)
    terms = terms_of(offsets, early_ref, so_ref, s_ref, ro_ref, rr_ref, block)
    own_ref[...] = terms[0]
    for offset, term, out in zip(offsets[1:], terms[1:], out_refs):
        ok = permitted(prof_ref, nblocks, position, position + offset)
        first, count = FIRST_COLUMN[offset], columns_to(offset)
        for c, tile in enumerate(placed_terms(ok, term, offset, first, count, block, F32)):
            out[:, c * block : (c + 1) * block] = tile


def combine_kernel(at_ref, pack_ref, own_ref, u2_ref, d2_ref, u4_ref, d4_ref, *outs):
    block = own_ref.shape[0]
    ins = {0: own_ref, 2: u2_ref, -2: d2_ref, 4: u4_ref, -4: d4_ref}
    to = dict(zip((0, 2, -2, 4, -4), outs))
    odd = lax.rem(at_ref[0], 2) == 1

    def merge(sources):
        for offset, out in to.items():
            first = 0 if offset == 0 else FIRST_COLUMN[offset]
            for c in range(out.shape[1] // block):
                columns = slice(c * block, (c + 1) * block)
                value = ins[offset][:, columns]
                if offset in sources:
                    n = sources[offset]
                    at = c + first - FIRST_COLUMN[ODD[n]]
                    if 0 <= at < 8:
                        tile = pack_ref[n, :, at * block : (at + 1) * block]
                        value = value + tile.astype(F32)
                out[:, columns] = value.astype(out.dtype)

    @pl.when(jnp.logical_not(odd))
    def _():
        merge({-2: 0, 0: 1, 2: 2, 4: 3})

    @pl.when(odd)
    def _():
        merge({-4: 0, -2: 1, 0: 2, 2: 3})


def gather_kernel(at_ref, own_ref, u2_ref, d2_ref, u4_ref, d4_ref, keep_ref, send_ref):
    block = own_ref.shape[0]
    rows = keep_ref.shape[0]
    half = at_ref[1]
    parts = {2: u2_ref, -2: d2_ref, 4: u4_ref, -4: d4_ref}
    for target, which in ((send_ref, 1 - half), (keep_ref, half)):
        window = pl.ds(pl.multiple_of(which * rows, rows), rows)
        for c in range(SLOTS):
            columns = slice(c * block, (c + 1) * block)
            total = own_ref[window, columns]
            for offset, part in parts.items():
                at = c - FIRST_COLUMN[offset]
                if 0 <= at < columns_to(offset):
                    total = total + part[window, at * block : (at + 1) * block].astype(F32)
            target[:, columns] = total.astype(target.dtype)


def finish_kernel(nblocks, block, scale, at_ref, prof_ref, keep_ref, got_ref, out_ref):
    position = at_ref[0]
    for c in range(SLOTS):
        columns = slice(c * block, (c + 1) * block)
        ok = permitted(prof_ref, nblocks, position, position + c - SPREAD)
        value = (keep_ref[:, columns] + got_ref[:, columns].astype(F32)) * scale
        out_ref[:, columns] = jnp.where(ok, value, jnp.zeros_like(value))


def gram_of(size, x_ref, quads, total):
    half = size // 2
    for s_ref, co_ref, po_ref, pr_ref in quads:
        got = dot(s_ref[...], x_ref[...]).astype(BF16)
        for g in range(s_ref.shape[0] // half):
            rows = slice(g * half, (g + 1) * half)
            coupled = jnp.concatenate([co_ref[rows, :], got[rows]], 0)
            partner = jnp.concatenate([po_ref[rows, :], pr_ref[rows, :]], 0)
            part = dot_columns(coupled, partner)
            total = part if total is None else total + part
    return total


def gram_kernel(count, x_ref, *refs):
    quads = [refs[4 * c : 4 * c + 4] for c in range(count)]
    out_ref = refs[4 * count]
    out_ref[...] = gram_of(out_ref.shape[0], x_ref, quads, None)


def polar_kernel(at_ref, x_ref, s_ref, co_ref, po_ref, pr_ref, gram_ref, mine_ref, theirs_ref, keep_ref, send_ref):
    size = gram_ref.shape[0]
    here, every = keep_ref.shape
    total = gram_of(size, x_ref, [(s_ref, co_ref, po_ref, pr_ref)], gram_ref[...])
    by_row = jnp.sum(jnp.where(same_row(size), total, 0.0).reshape(every, SUB, size), 1)
    polar = jnp.dot(
        by_row, one_hot(size, every), preferred_element_type=F32, precision=lax.Precision.HIGHEST
    )
    row, alive = screen_row(mine_ref, theirs_ref)
    polar = polar * row * alive
    turned = jnp.concatenate([polar[:, here:], polar[:, :here]], 1)
    polar = jnp.where(at_ref[1] == 0, polar, turned)
    keep_ref[...] = polar[:here]
    send_ref[...] = polar[here:]


def step(occupied, virtual, three_centre, kernel, profile, atom_map):
    block, width = occupied.shape
    nblocks = lax.axis_size("chain")
    halves = lax.axis_size("aux")
    if halves != 2 or width != SLOTS * block or nblocks % 2:
        raise ValueError("unsupported mesh")
    position = lax.axis_index("chain")
    half = lax.axis_index("aux")
    here = three_centre.shape[0]
    every = kernel.shape[1]
    rows = block // halves
    groups = rows // SUB
    per_group = here * SUB
    per_chunk = groups // CHUNKS
    span = per_chunk * per_group
    at = jnp.stack([position, half]).astype(jnp.int32)

    def cut(picks, grant=24):
        shape = (per_chunk, here, SUB, width)
        call = pl.pallas_call(
            functools.partial(cut_kernel, rows, picks),
            out_shape=[shaped(shape)] * len(picks),
            in_specs=[SMEM, pl.BlockSpec(memory_space=pltpu.HBM)],
            out_specs=[VMEM] * len(picks),
            scratch_shapes=[pltpu.SemaphoreType.DMA((len(picks) * per_chunk,))],
            compiler_params=pltpu.CompilerParams(vmem_limit_bytes=grant * 1024 * 1024),
            cost_estimate=pl.CostEstimate(
                flops=0, bytes_accessed=4 * len(picks) * span * width, transcendentals=0
            ),
        )
        return [part.reshape(span, width) for part in call(at, three_centre)]

    def halo(band):
        mid = swapped(band, "chain")
        packs = run(
            pair_kernel,
            [at, band, mid],
            [shaped((block, 15 * block)), shaped((block, 11 * block))],
            smem=1,
        )
        hops = []
        for distance, pack in zip((2, 4), packs):
            up = [(i, i + distance) for i in range(0, nblocks - distance, 2)]
            down = [(i + distance, i) for i in range(1, nblocks - distance, 2)]
            hops.append(lax.ppermute(pack, "chain", up + down))
        return [band, mid, *hops, *[swapped(h, "chain") for h in hops]]

    starts = [c * per_chunk for c in range(CHUNKS)]
    sends = cut([(False, starts[0])])
    rest = cut([(False, f) for f in starts[1:]] + [(True, f) for f in starts])
    sends += rest[: CHUNKS - 1]
    own = rest[CHUNKS - 1 :]
    got = [swapped(part, "aux") for part in sends]
    near_vir = halo(virtual)
    near_occ = halo(occupied)

    mine, send = run(
        functools.partial(prepare_kernel, nblocks),
        [at, atom_map, kernel],
        [shaped((here, 2 * every), F32)] * 2,
        smem=2,
    )
    theirs = swapped(send, "aux")

    product = 2 * span * width * width
    vir_stack, *partner_own = run(
        functools.partial(stack_kernel, nblocks, CHUNKS),
        [at, profile, *near_vir, *own],
        [shaped((width, width))] + [shaped((span, width))] * CHUNKS,
        flops=CHUNKS * product,
        smem=2,
    )
    partner_got, resp_own, resp_got = [], [], []
    for c in range(CHUNKS - 1):
        pr, ro, rr = run(
            respond_kernel,
            [mine, theirs, vir_stack, got[c], partner_own[c]],
            [shaped((span, width))] * 3,
            flops=2 * product,
        )
        partner_got.append(pr)
        resp_own.append(ro)
        resp_got.append(rr)
    (early,) = run(
        functools.partial(early_kernel, 2 * (CHUNKS - 1)),
        [*own[:-1], *got[:-1], *resp_own, *resp_got],
        [shaped((width, width), F32)],
        flops=2 * (CHUNKS - 1) * product,
    )
    pr, ro, rr, pack = run(
        functools.partial(odd_kernel, nblocks),
        [at, profile, mine, theirs, vir_stack, got[-1], partner_own[-1], own[-1], early],
        [shaped((span, width))] * 3 + [shaped((len(ODD), block, 8 * block))],
        flops=2 * product,
        smem=2,
    )
    partner_got.append(pr)
    other_pack = swapped(pack, "chain")
    offsets = (2, -2, 4, -4)
    even = run(
        functools.partial(even_kernel, nblocks),
        [at, profile, own[-1], got[-1], ro, rr, early],
        [shaped((block, width), F32)]
        + [shaped((block, columns_to(d) * block), F32) for d in offsets],
        flops=product,
        smem=2,
    )
    mid, *sends = run(
        combine_kernel,
        [at, other_pack, *even],
        [shaped((block, width), F32)] + [shaped((block, columns_to(d) * block)) for d in offsets],
        smem=1,
    )
    arrived = [passed_along(s, "chain", d) for s, d in zip(sends, offsets)]
    keep, send = run(
        gather_kernel,
        [at, mid, *arrived],
        [shaped((rows, width), F32), shaped((rows, width))],
        smem=1,
    )
    (band_gradient,) = run(
        functools.partial(finish_kernel, nblocks, block, 1.0 / math.sqrt(block * every)),
        [at, profile, keep, swapped(send, "aux")],
        [shaped((rows, width), F32)],
        smem=2,
    )

    occ_stack, *coupled_own = run(
        functools.partial(stack_kernel, nblocks, CHUNKS),
        [at, profile, *near_occ, *own],
        [shaped((width, width))] + [shaped((span, width))] * CHUNKS,
        flops=CHUNKS * product,
        smem=2,
    )
    size = every * SUB
    quads = [q for c in range(CHUNKS - 1) for q in (got[c], coupled_own[c], partner_own[c], partner_got[c])]
    (gram,) = run(
        functools.partial(gram_kernel, CHUNKS - 1),
        [occ_stack, *quads],
        [shaped((size, size), F32)],
        flops=CHUNKS * product,
    )
    polar, send = run(
        polar_kernel,
        [at, occ_stack, got[-1], coupled_own[-1], partner_own[-1], partner_got[-1], gram, mine, theirs],
        [shaped((here, every), F32)] * 2,
        flops=2 * product,
        smem=1,
    )
    polar = polar + swapped(send, "aux")
    bit = 1
    while bit < nblocks:
        polar = polar + swapped(polar, "chain", bit)
        bit *= 2
    polarization = polar * (1.0 / math.sqrt(block * nblocks * width))
    return (band_gradient, polarization)


def solution(mesh):
    placed = (
        P("chain", None),
        P("chain", None),
        P("aux", "chain", None),
        P("aux", None),
        P(),
        P("aux"),
    )
    return jax.shard_map(
        step,
        mesh=mesh,
        in_specs=placed,
        out_specs=(P(("chain", "aux"), None), P("aux", None)),
        check_vma=False,
    )
```

```python
import functools
import math

import jax
import jax.numpy as jnp
from jax import lax
from jax.experimental import pallas as pl
from jax.experimental.pallas import tpu as pltpu
from jax.sharding import PartitionSpec as P


F32 = jnp.float32
BF16 = jnp.bfloat16
SUB = 8
SPREAD = 4
SLOTS = 9
VMEM = pl.BlockSpec(memory_space=pltpu.VMEM)
SMEM = pl.BlockSpec(memory_space=pltpu.SMEM)
FIRST_COLUMN = {2: 0, -2: 1, 4: 0, -4: 3, 1: 0, 3: 0, -1: 1, -3: 1}
ODD = (-3, -1, 1, 3)


def columns_to(offset):
    return 6 if abs(offset) == 4 else 8


def passed_along(block, axis, distance):
    devices = range(lax.axis_size(axis))
    route = [(i - distance, i) for i in devices if i - distance in devices]
    return lax.ppermute(block, axis, route)


def swapped(block, axis, bit=1):
    return lax.ppermute(block, axis, [(i, i ^ bit) for i in range(lax.axis_size(axis))])


def permitted(prof_ref, nblocks, a, b):
    last = nblocks - 1
    inside = (a >= 0) & (a <= last) & (b >= 0) & (b <= last)
    wide_a = prof_ref[jnp.clip(a, 0, last)]
    wide_b = prof_ref[jnp.clip(b, 0, last)]
    return inside & (jnp.abs(a - b) <= jnp.minimum(wide_a, wide_b))


def run(kernel, operands, outs, flops=0, smem=0, grant=24):
    nbytes = sum(math.prod(s.shape) * s.dtype.itemsize for s in (*operands, *outs))
    return pl.pallas_call(
        kernel,
        out_shape=outs,
        in_specs=[SMEM] * smem + [VMEM] * (len(operands) - smem),
        out_specs=[VMEM] * len(outs),
        compiler_params=pltpu.CompilerParams(vmem_limit_bytes=grant * 1024 * 1024),
        cost_estimate=pl.CostEstimate(
            flops=int(flops), bytes_accessed=int(nbytes), transcendentals=0
        ),
    )(*operands)


def shaped(shape, dtype=BF16):
    return jax.ShapeDtypeStruct(shape, dtype)


def dot(a, b):
    return jnp.dot(a, b, preferred_element_type=F32)


def dot_rows(a, b):
    return lax.dot_general(a, b, (((0,), (0,)), ((), ())), preferred_element_type=F32)


def dot_columns(a, b):
    return lax.dot_general(a, b, (((1,), (1,)), ((), ())), preferred_element_type=F32)


def prepare_kernel(nblocks, at_ref, atom_ref, k_ref, keep_ref, send_ref):
    here, every = k_ref.shape
    position, half = at_ref[0], at_ref[1]
    rows = lax.broadcasted_iota(jnp.int32, (here, every), 0)
    alive = jnp.zeros((here, every), F32)
    for p in range(here):
        near = jnp.abs(atom_ref[p] - position) <= nblocks // 4
        alive = jnp.where((rows == p) & near, 1.0, alive)
    plain = k_ref[...].astype(F32) * alive
    turned = jnp.concatenate([plain[:, here:], plain[:, :here]], 1)
    keep_ref[:, :every] = jnp.where(half == 0, plain, turned)
    keep_ref[:, every:] = alive
    send_ref[:, :every] = jnp.where(half == 0, turned, plain)
    send_ref[:, every:] = alive


def screen_row(mine_ref, theirs_ref):
    every = mine_ref.shape[1] // 2
    alive = jnp.concatenate([mine_ref[:, every:], theirs_ref[:, every:]], 0)
    r = lax.broadcasted_iota(jnp.int32, (every, every), 0)
    c = lax.broadcasted_iota(jnp.int32, (every, every), 1)
    return jnp.sum(jnp.where(r == c, alive, 0.0), 0, keepdims=True), alive


def one_hot(rows, cols):
    r = lax.broadcasted_iota(jnp.int32, (rows, cols), 0)
    c = lax.broadcasted_iota(jnp.int32, (rows, cols), 1)
    return (r // SUB == c).astype(F32)


def same_row(size):
    r = lax.broadcasted_iota(jnp.int32, (size, size), 0)
    c = lax.broadcasted_iota(jnp.int32, (size, size), 1)
    return lax.rem(r, SUB) == lax.rem(c, SUB)


def mixing_kernel(mine_ref, theirs_ref, out_ref):
    every = mine_ref.shape[1] // 2
    size = every * SUB
    row, _ = screen_row(mine_ref, theirs_ref)
    k = jnp.concatenate([mine_ref[:, :every], theirs_ref[:, :every]], 0) * row
    pick = one_hot(size, every).astype(BF16)
    wide = dot_columns(dot(pick, k.astype(BF16)).astype(BF16), pick)
    out_ref[...] = jnp.where(same_row(size), wide, 0.0).astype(BF16)


def band_slots(delta, which):
    sizes = {1: (7, 8), 2: (5, 6), -1: (8, 7), -2: (6, 5)}[delta]
    count = sizes[which]
    first = SLOTS - count if delta > 0 else 0
    return first, count, sizes[0] * which


def pair_kernel(at_ref, own_ref, mid_ref, out1_ref, out2_ref):
    block = own_ref.shape[0]

    def fill(sign, pair):
        for distance, out in ((1, out1_ref), (2, out2_ref)):
            for which in range(2):
                first, count, start = band_slots(sign * distance, which)
                out[:, start * block : (start + count) * block] = pair[which][
                    :, first * block : (first + count) * block
                ]

    odd = lax.rem(at_ref[0], 2) == 1

    @pl.when(jnp.logical_not(odd))
    def _():
        fill(1, (own_ref, mid_ref))

    @pl.when(odd)
    def _():
        fill(-1, (mid_ref, own_ref))


def stack_kernel(nblocks, at_ref, prof_ref, *refs):
    own_ref, mid_ref, hop1_ref, hop2_ref, near1_ref, near2_ref = refs[:6]
    rows_ref, stack_ref, out_ref = refs[6:]
    block = own_ref.shape[0]
    position = at_ref[0]

    def build(parity, pair, below, above):
        for offset in range(-SPREAD, SPREAD + 1):
            delta, which = divmod(parity + offset, 2)
            rows = slice((offset + SPREAD) * block, (offset + SPREAD + 1) * block)
            other = position + offset
            row_ok = permitted(prof_ref, nblocks, position, other)
            for col in range(SLOTS):
                slot = col - offset
                columns = slice(col * block, (col + 1) * block)
                if not 0 <= slot < SLOTS:
                    stack_ref[rows, columns] = jnp.zeros((block, block), BF16)
                    continue
                if delta == 0:
                    source, at = pair[which], slot
                else:
                    first, _, start = band_slots(-delta, which)
                    source = (below if delta < 0 else above)[abs(delta) - 1]
                    at = start + slot - first
                ok = row_ok & permitted(prof_ref, nblocks, other, position + col - SPREAD)
                tile = source[:, at * block : (at + 1) * block]
                stack_ref[rows, columns] = jnp.where(ok, tile, jnp.zeros_like(tile))

    odd = lax.rem(position, 2) == 1
    hops, nears = (hop1_ref, hop2_ref), (near1_ref, near2_ref)

    @pl.when(jnp.logical_not(odd))
    def _():
        build(0, (own_ref, mid_ref), hops, nears)

    @pl.when(odd)
    def _():
        build(1, (mid_ref, own_ref), nears, hops)

    part = out_ref.shape[0] // 4
    for n in range(4):
        rows = slice(n * part, (n + 1) * part)
        out_ref[rows, :] = dot(rows_ref[rows, :], stack_ref[...]).astype(BF16)


def cut_kernel(rows, picks, at_ref, three_ref, *refs):
    outs, sem = refs[:-1], refs[-1]
    copies = []
    for (mine, first), out in zip(picks, outs):
        which = at_ref[1] if mine else 1 - at_ref[1]
        for g in range(out.shape[0]):
            start = pl.multiple_of(which * rows + (first + g) * SUB, SUB)
            copies.append(
                pltpu.make_async_copy(
                    three_ref.at[:, pl.ds(start, SUB), :], out.at[g], sem.at[len(copies)]
                )
            )
    for copy in copies:
        copy.start()
    for copy in copies:
        copy.wait()


def respond_kernel(first, mixed_ref, v_ref, s_ref, po_ref, pr_ref, resp_ref):
    pr_ref[...] = dot(s_ref[...], v_ref[...]).astype(BF16)
    half = mixed_ref.shape[0] // 2
    span = s_ref.shape[0]
    for g in range(span // half):
        rows = slice(g * half, (g + 1) * half)
        own_rows = slice(first + g * half, first + (g + 1) * half)
        partner = jnp.concatenate([po_ref[own_rows, :], pr_ref[rows, :]], 0)
        resp = dot(mixed_ref[...], partner).astype(BF16)
        resp_ref[rows, :] = resp[:half]
        resp_ref[span + g * half : span + (g + 1) * half, :] = resp[half:]


def early_kernel(spans, so_ref, *refs):
    count = len(spans)
    out_ref = refs[-1]
    third = out_ref.shape[0] // 3
    for m in range(3):
        cols = slice(m * third, (m + 1) * third)
        acc = None
        for rows, s_ref, resp_ref in zip(spans, refs[:count], refs[count:]):
            both = jnp.concatenate([so_ref[rows, cols], s_ref[:, cols]], 0)
            part = dot_rows(both, resp_ref[...])
            acc = part if acc is None else acc + part
        out_ref[cols, :] = acc


def terms_of(offsets, first, early_ref, so_ref, sr_ref, resp_ref, block):
    take = [slice((d + SPREAD) * block, (d + SPREAD + 1) * block) for d in offsets]
    rows = slice(first, first + sr_ref.shape[0])
    both = [jnp.concatenate([so_ref[rows, t], sr_ref[:, t]], 0) for t in take]
    total = dot_rows(jnp.concatenate(both, 1), resp_ref[...])
    return [total[n * block : (n + 1) * block] + early_ref[t, :] for n, t in enumerate(take)]


def placed_terms(ok, term, offset, first, count, block, dtype):
    tiles = []
    for c in range(first, first + count):
        source = c + offset
        if 0 <= source < SLOTS:
            tile = term[:, source * block : (source + 1) * block]
            tiles.append(jnp.where(ok, tile, jnp.zeros_like(tile)).astype(dtype))
        else:
            tiles.append(jnp.zeros((block, block), dtype))
    return tiles


def odd_kernel(
    nblocks, first, at_ref, prof_ref, mixed_ref, v_ref, s_ref, po_ref, so_ref, early_ref,
    pr_ref, resp_ref, pack_ref,
):
    respond_kernel(first, mixed_ref, v_ref, s_ref, po_ref, pr_ref, resp_ref)
    block = pack_ref.shape[1]
    position = at_ref[0]
    terms = terms_of(ODD, first, early_ref, so_ref, s_ref, resp_ref, block)
    for n, (offset, term) in enumerate(zip(ODD, terms)):
        ok = permitted(prof_ref, nblocks, position, position + offset)
        tiles = placed_terms(ok, term, offset, FIRST_COLUMN[offset], 8, block, BF16)
        for c, tile in enumerate(tiles):
            pack_ref[n, :, c * block : (c + 1) * block] = tile


def even_kernel(
    nblocks, first, at_ref, prof_ref, so_ref, s_ref, resp_ref, early_ref, own_ref, *out_refs
):
    block = own_ref.shape[0]
    position = at_ref[0]
    offsets = (0, 2, -2, 4, -4)
    terms = terms_of(offsets, first, early_ref, so_ref, s_ref, resp_ref, block)
    own_ref[...] = terms[0]
    for offset, term, out in zip(offsets[1:], terms[1:], out_refs):
        ok = permitted(prof_ref, nblocks, position, position + offset)
        begin, count = FIRST_COLUMN[offset], columns_to(offset)
        for c, tile in enumerate(placed_terms(ok, term, offset, begin, count, block, F32)):
            out[:, c * block : (c + 1) * block] = tile


def combine_kernel(at_ref, pack_ref, own_ref, u2_ref, d2_ref, u4_ref, d4_ref, *outs):
    block = own_ref.shape[0]
    ins = {0: own_ref, 2: u2_ref, -2: d2_ref, 4: u4_ref, -4: d4_ref}
    to = dict(zip((0, 2, -2, 4, -4), outs))
    odd = lax.rem(at_ref[0], 2) == 1

    def merge(sources):
        for offset, out in to.items():
            first = 0 if offset == 0 else FIRST_COLUMN[offset]
            for c in range(out.shape[1] // block):
                columns = slice(c * block, (c + 1) * block)
                value = ins[offset][:, columns]
                if offset in sources:
                    n = sources[offset]
                    at = c + first - FIRST_COLUMN[ODD[n]]
                    if 0 <= at < 8:
                        tile = pack_ref[n, :, at * block : (at + 1) * block]
                        value = value + tile.astype(F32)
                out[:, columns] = value.astype(out.dtype)

    @pl.when(jnp.logical_not(odd))
    def _():
        merge({-2: 0, 0: 1, 2: 2, 4: 3})

    @pl.when(odd)
    def _():
        merge({-4: 0, -2: 1, 0: 2, 2: 3})


def gather_kernel(at_ref, own_ref, u2_ref, d2_ref, u4_ref, d4_ref, keep_ref, send_ref):
    block = own_ref.shape[0]
    rows = keep_ref.shape[0]
    half = at_ref[1]
    parts = {2: u2_ref, -2: d2_ref, 4: u4_ref, -4: d4_ref}
    for target, which in ((send_ref, 1 - half), (keep_ref, half)):
        window = pl.ds(pl.multiple_of(which * rows, rows), rows)
        for c in range(SLOTS):
            columns = slice(c * block, (c + 1) * block)
            total = own_ref[window, columns]
            for offset, part in parts.items():
                at = c - FIRST_COLUMN[offset]
                if 0 <= at < columns_to(offset):
                    total = total + part[window, at * block : (at + 1) * block].astype(F32)
            target[:, columns] = total.astype(target.dtype)


def finish_kernel(
    nblocks, block, scale, polar_scale, at_ref, prof_ref, keep_ref, got_ref, pk_ref, pg_ref,
    out_ref, polar_ref,
):
    polar_ref[...] = (pk_ref[...] + pg_ref[...]) * polar_scale
    position = at_ref[0]
    for c in range(SLOTS):
        columns = slice(c * block, (c + 1) * block)
        ok = permitted(prof_ref, nblocks, position, position + c - SPREAD)
        value = (keep_ref[:, columns] + got_ref[:, columns].astype(F32)) * scale
        out_ref[:, columns] = jnp.where(ok, value, jnp.zeros_like(value))


def gram_of(size, x_ref, co_ref, po_ref, chunks, total):
    half = size // 2
    for first, s_ref, pr_ref in chunks:
        got = dot(s_ref[...], x_ref[...]).astype(BF16)
        for g in range(s_ref.shape[0] // half):
            rows = slice(g * half, (g + 1) * half)
            own_rows = slice(first + g * half, first + (g + 1) * half)
            coupled = jnp.concatenate([co_ref[own_rows, :], got[rows]], 0)
            partner = jnp.concatenate([po_ref[own_rows, :], pr_ref[rows, :]], 0)
            part = dot_columns(coupled, partner)
            total = part if total is None else total + part
    return total


def chunk_refs(firsts, refs):
    return list(zip(firsts, refs[::2], refs[1::2]))


def gram_kernel(firsts, x_ref, co_ref, po_ref, *refs):
    out_ref = refs[-1]
    chunks = chunk_refs(firsts, refs[:-1])
    out_ref[...] = gram_of(out_ref.shape[0], x_ref, co_ref, po_ref, chunks, None)


def polar_kernel(firsts, at_ref, x_ref, co_ref, po_ref, gram_ref, mine_ref, theirs_ref, *refs):
    out_ref = refs[-1]
    size = gram_ref.shape[0]
    every = out_ref.shape[0]
    here = every // 2
    chunks = chunk_refs(firsts, refs[:-1])
    total = gram_of(size, x_ref, co_ref, po_ref, chunks, gram_ref[...])
    by_row = jnp.sum(jnp.where(same_row(size), total, 0.0).reshape(every, SUB, size), 1)
    polar = jnp.dot(
        by_row, one_hot(size, every), preferred_element_type=F32, precision=lax.Precision.HIGHEST
    )
    row, alive = screen_row(mine_ref, theirs_ref)
    polar = polar * row * alive
    turned = jnp.concatenate([polar[:, here:], polar[:, :here]], 1)
    out_ref[...] = jnp.where(at_ref[1] == 0, polar, turned)


def step(occupied, virtual, three_centre, kernel, profile, atom_map):
    block, width = occupied.shape
    nblocks = lax.axis_size("chain")
    halves = lax.axis_size("aux")
    if halves != 2 or width != SLOTS * block or nblocks % 2:
        raise ValueError("unsupported mesh")
    position = lax.axis_index("chain")
    half = lax.axis_index("aux")
    here = three_centre.shape[0]
    every = kernel.shape[1]
    rows = block // halves
    groups = rows // SUB
    per_group = here * SUB
    most = -(-groups // 3)
    sizes = (most, most, groups - 2 * most)
    begins = (0, most, 2 * most)
    firsts = [g * per_group for g in begins]
    counts = [g * per_group for g in sizes]
    at = jnp.stack([position, half]).astype(jnp.int32)

    integrals = pltpu.with_memory_space_constraint(three_centre, pltpu.HBM)

    def cut(picks):
        lengths = [count for _, _, count in picks]
        call = pl.pallas_call(
            functools.partial(cut_kernel, rows, [pick[:2] for pick in picks]),
            out_shape=[shaped((count, here, SUB, width)) for count in lengths],
            in_specs=[SMEM, pl.BlockSpec(memory_space=pltpu.HBM)],
            out_specs=[VMEM] * len(picks),
            scratch_shapes=[pltpu.SemaphoreType.DMA((sum(lengths),))],
            compiler_params=pltpu.CompilerParams(vmem_limit_bytes=24 * 1024 * 1024),
            cost_estimate=pl.CostEstimate(
                flops=0, bytes_accessed=4 * sum(lengths) * per_group * width, transcendentals=0
            ),
        )
        parts = call(at, integrals)
        return [part.reshape(-1, width) for part in parts]

    def halo(band):
        mid = swapped(band, "chain")
        packs = run(
            pair_kernel,
            [at, band, mid],
            [shaped((block, 15 * block)), shaped((block, 11 * block))],
            smem=1,
        )
        hops = []
        for distance, pack in zip((2, 4), packs):
            up = [(i, i + distance) for i in range(0, nblocks - distance, 2)]
            down = [(i + distance, i) for i in range(1, nblocks - distance, 2)]
            hops.append(lax.ppermute(pack, "chain", up + down))
        return [band, mid, *hops, *[swapped(h, "chain") for h in hops]]

    sends = cut([(False, begins[0], sizes[0])])
    rest = [(False, f, n) for f, n in zip(begins[1:], sizes[1:])]
    *others, own = cut(rest + [(True, 0, groups)])
    got = [swapped(part, "aux") for part in [*sends, *others]]
    near_vir = halo(virtual)
    near_occ = halo(occupied)

    mine, send = run(
        functools.partial(prepare_kernel, nblocks),
        [at, atom_map, kernel],
        [shaped((here, 2 * every), F32)] * 2,
        smem=2,
    )
    theirs = swapped(send, "aux")

    (mixed,) = run(mixing_kernel, [mine, theirs], [shaped((every * SUB, every * SUB))])

    per_row = 2 * width * width
    own_flops = own.shape[0] * per_row

    def contracted(near):
        return run(
            functools.partial(stack_kernel, nblocks),
            [at, profile, *near, own],
            [shaped((width, width)), shaped(own.shape)],
            flops=own_flops,
            smem=2,
        )

    vir_stack, partner_own = contracted(near_vir)
    partner_got, responses = [], []
    for c in range(2):
        pr, resp = run(
            functools.partial(respond_kernel, firsts[c]),
            [mixed, vir_stack, got[c], partner_own],
            [shaped((counts[c], width)), shaped((2 * counts[c], width))],
            flops=2 * counts[c] * per_row,
        )
        partner_got.append(pr)
        responses.append(resp)
    (early,) = run(
        functools.partial(early_kernel, [slice(f, f + n) for f, n in zip(firsts[:2], counts)]),
        [own, *got[:2], *responses],
        [shaped((width, width), F32)],
        flops=2 * firsts[2] * per_row,
    )
    pr, resp, pack = run(
        functools.partial(odd_kernel, nblocks, firsts[2]),
        [at, profile, mixed, vir_stack, got[2], partner_own, own, early],
        [
            shaped((counts[2], width)),
            shaped((2 * counts[2], width)),
            shaped((len(ODD), block, 8 * block)),
        ],
        flops=2 * counts[2] * per_row,
        smem=2,
    )
    partner_got.append(pr)
    other_pack = swapped(pack, "chain")
    offsets = (2, -2, 4, -4)
    even = run(
        functools.partial(even_kernel, nblocks, firsts[2]),
        [at, profile, own, got[2], resp, early],
        [shaped((block, width), F32)]
        + [shaped((block, columns_to(d) * block), F32) for d in offsets],
        flops=counts[2] * per_row,
        smem=2,
    )
    mid, *sends = run(
        combine_kernel,
        [at, other_pack, *even],
        [shaped((block, width), F32)] + [shaped((block, columns_to(d) * block)) for d in offsets],
        smem=1,
    )
    arrived = [passed_along(s, "chain", d) for s, d in zip(sends, offsets)]
    keep, send = run(
        gather_kernel,
        [at, mid, *arrived],
        [shaped((rows, width), F32), shaped((rows, width))],
        smem=1,
    )
    occ_stack, coupled_own = contracted(near_occ)
    size = every * SUB
    (gram,) = run(
        functools.partial(gram_kernel, firsts[:2]),
        [occ_stack, coupled_own, partner_own, got[0], partner_got[0], got[1], partner_got[1]],
        [shaped((size, size), F32)],
        flops=firsts[2] * per_row,
    )
    (polar,) = run(
        functools.partial(polar_kernel, firsts[2:]),
        [at, occ_stack, coupled_own, partner_own, gram, mine, theirs, got[2], partner_got[2]],
        [shaped((every, every), F32)],
        flops=counts[2] * per_row,
        smem=1,
    )
    bits = [1 << n for n in range(nblocks.bit_length() - 1)]
    first = bits.pop(min(2, len(bits) - 1))
    polar = polar + swapped(polar, "chain", first)
    polar = polar[:here] + swapped(polar[here:], "aux")
    for n, bit in enumerate(bits):
        other = swapped(polar, "chain", bit)
        if n < len(bits) - 1:
            polar = polar + other
    return run(
        functools.partial(
            finish_kernel,
            nblocks,
            block,
            1.0 / math.sqrt(block * every),
            1.0 / math.sqrt(block * nblocks * width),
        ),
        [at, profile, keep, swapped(send, "aux"), polar, other],
        [shaped((rows, width), F32), shaped((here, every), F32)],
        smem=2,
    )


def solution(mesh):
    placed = (
        P("chain", None),
        P("chain", None),
        P("aux", "chain", None),
        P("aux", None),
        P(),
        P("aux"),
    )
    return jax.shard_map(
        step,
        mesh=mesh,
        in_specs=placed,
        out_specs=(P(("chain", "aux"), None), P("aux", None)),
        check_vma=False,
    )
```

```python
import functools
import math

import jax
import jax.numpy as jnp
from jax import lax
from jax.experimental import pallas as pl
from jax.experimental.pallas import tpu as pltpu
from jax.sharding import PartitionSpec as P


F32 = jnp.float32
BF16 = jnp.bfloat16
SUB = 8
SPREAD = 4
SLOTS = 9
VMEM = pl.BlockSpec(memory_space=pltpu.VMEM)
SMEM = pl.BlockSpec(memory_space=pltpu.SMEM)
FIRST_COLUMN = {2: 0, -2: 1, 4: 0, -4: 3, 1: 0, 3: 0, -1: 1, -3: 1}
ODD = (-3, -1, 1, 3)


def columns_to(offset):
    return 6 if abs(offset) == 4 else 8


def swapped(block, axis, bit=1):
    return lax.ppermute(block, axis, [(i, i ^ bit) for i in range(lax.axis_size(axis))])


def permitted(prof_ref, nblocks, a, b):
    last = nblocks - 1
    inside = (a >= 0) & (a <= last) & (b >= 0) & (b <= last)
    wide_a = prof_ref[jnp.clip(a, 0, last)]
    wide_b = prof_ref[jnp.clip(b, 0, last)]
    return inside & (jnp.abs(a - b) <= jnp.minimum(wide_a, wide_b))


def run(kernel, operands, outs, flops=0, smem=0, grant=24):
    nbytes = sum(math.prod(s.shape) * s.dtype.itemsize for s in (*operands, *outs))
    return pl.pallas_call(
        kernel,
        out_shape=outs,
        in_specs=[SMEM] * smem + [VMEM] * (len(operands) - smem),
        out_specs=[VMEM] * len(outs),
        compiler_params=pltpu.CompilerParams(vmem_limit_bytes=grant * 1024 * 1024),
        cost_estimate=pl.CostEstimate(
            flops=int(flops), bytes_accessed=int(nbytes), transcendentals=0
        ),
    )(*operands)


def shaped(shape, dtype=BF16):
    return jax.ShapeDtypeStruct(shape, dtype)


def dot(a, b):
    return jnp.dot(a, b, preferred_element_type=F32)


def dot_rows(a, b):
    return lax.dot_general(a, b, (((0,), (0,)), ((), ())), preferred_element_type=F32)


def dot_columns(a, b):
    return lax.dot_general(a, b, (((1,), (1,)), ((), ())), preferred_element_type=F32)


def prepare_kernel(nblocks, at_ref, atom_ref, k_ref, keep_ref, send_ref):
    here, every = k_ref.shape
    position, half = at_ref[0], at_ref[1]
    rows = lax.broadcasted_iota(jnp.int32, (here, every), 0)
    alive = jnp.zeros((here, every), F32)
    for p in range(here):
        near = jnp.abs(atom_ref[p] - position) <= nblocks // 4
        alive = jnp.where((rows == p) & near, 1.0, alive)
    plain = k_ref[...].astype(F32) * alive
    turned = jnp.concatenate([plain[:, here:], plain[:, :here]], 1)
    keep_ref[:, :every] = jnp.where(half == 0, plain, turned)
    keep_ref[:, every:] = alive
    send_ref[:, :every] = jnp.where(half == 0, turned, plain)
    send_ref[:, every:] = alive


def screen_row(mine_ref, theirs_ref):
    every = mine_ref.shape[1] // 2
    alive = jnp.concatenate([mine_ref[:, every:], theirs_ref[:, every:]], 0)
    r = lax.broadcasted_iota(jnp.int32, (every, every), 0)
    c = lax.broadcasted_iota(jnp.int32, (every, every), 1)
    return jnp.sum(jnp.where(r == c, alive, 0.0), 0, keepdims=True), alive


def one_hot(rows, cols):
    r = lax.broadcasted_iota(jnp.int32, (rows, cols), 0)
    c = lax.broadcasted_iota(jnp.int32, (rows, cols), 1)
    return (r // SUB == c).astype(F32)


def same_row(size):
    r = lax.broadcasted_iota(jnp.int32, (size, size), 0)
    c = lax.broadcasted_iota(jnp.int32, (size, size), 1)
    return lax.rem(r, SUB) == lax.rem(c, SUB)


def mixing_kernel(mine_ref, theirs_ref, out_ref):
    every = mine_ref.shape[1] // 2
    size = every * SUB
    row, _ = screen_row(mine_ref, theirs_ref)
    k = jnp.concatenate([mine_ref[:, :every], theirs_ref[:, :every]], 0) * row
    pick = one_hot(size, every).astype(BF16)
    wide = dot_columns(dot(pick, k.astype(BF16)).astype(BF16), pick)
    out_ref[...] = jnp.where(same_row(size), wide, 0.0).astype(BF16)


def band_slots(delta, which):
    sizes = {1: (7, 8), 2: (5, 6), -1: (8, 7), -2: (6, 5)}[delta]
    count = sizes[which]
    first = SLOTS - count if delta > 0 else 0
    return first, count, sizes[0] * which


def pair_kernel(at_ref, own_ref, mid_ref, out1_ref, out2_ref):
    block = own_ref.shape[0]

    def fill(sign, pair):
        for distance, out in ((1, out1_ref), (2, out2_ref)):
            for which in range(2):
                first, count, start = band_slots(sign * distance, which)
                out[:, start * block : (start + count) * block] = pair[which][
                    :, first * block : (first + count) * block
                ]

    odd = lax.rem(at_ref[0], 2) == 1

    @pl.when(jnp.logical_not(odd))
    def _():
        fill(1, (own_ref, mid_ref))

    @pl.when(odd)
    def _():
        fill(-1, (mid_ref, own_ref))


def stack_kernel(nblocks, at_ref, prof_ref, *refs):
    own_ref, mid_ref, hop1_ref, hop2_ref, near1_ref, near2_ref = refs[:6]
    rows_ref, stack_ref, out_ref = refs[6:]
    block = own_ref.shape[0]
    position = at_ref[0]

    def build(parity, pair, below, above):
        for offset in range(-SPREAD, SPREAD + 1):
            delta, which = divmod(parity + offset, 2)
            rows = slice((offset + SPREAD) * block, (offset + SPREAD + 1) * block)
            other = position + offset
            row_ok = permitted(prof_ref, nblocks, position, other)
            for col in range(SLOTS):
                slot = col - offset
                columns = slice(col * block, (col + 1) * block)
                if not 0 <= slot < SLOTS:
                    stack_ref[rows, columns] = jnp.zeros((block, block), BF16)
                    continue
                if delta == 0:
                    source, at = pair[which], slot
                else:
                    first, _, start = band_slots(-delta, which)
                    source = (below if delta < 0 else above)[abs(delta) - 1]
                    at = start + slot - first
                ok = row_ok & permitted(prof_ref, nblocks, other, position + col - SPREAD)
                tile = source[:, at * block : (at + 1) * block]
                stack_ref[rows, columns] = jnp.where(ok, tile, jnp.zeros_like(tile))

    odd = lax.rem(position, 2) == 1
    hops, nears = (hop1_ref, hop2_ref), (near1_ref, near2_ref)

    @pl.when(jnp.logical_not(odd))
    def _():
        build(0, (own_ref, mid_ref), hops, nears)

    @pl.when(odd)
    def _():
        build(1, (mid_ref, own_ref), nears, hops)

    part = out_ref.shape[0] // 4
    for n in range(4):
        rows = slice(n * part, (n + 1) * part)
        out_ref[rows, :] = dot(rows_ref[rows, :], stack_ref[...]).astype(BF16)


def cut_kernel(rows, picks, at_ref, three_ref, *refs):
    outs, sem = refs[:-1], refs[-1]
    copies = []
    for (mine, first), out in zip(picks, outs):
        which = at_ref[1] if mine else 1 - at_ref[1]
        for g in range(out.shape[0]):
            start = pl.multiple_of(which * rows + (first + g) * SUB, SUB)
            copies.append(
                pltpu.make_async_copy(
                    three_ref.at[:, pl.ds(start, SUB), :], out.at[g], sem.at[len(copies)]
                )
            )
    for copy in copies:
        copy.start()
    for copy in copies:
        copy.wait()


def respond_kernel(first, mixed_ref, v_ref, s_ref, po_ref, pr_ref, resp_ref):
    pr_ref[...] = dot(s_ref[...], v_ref[...]).astype(BF16)
    half = mixed_ref.shape[0] // 2
    span = s_ref.shape[0]
    for g in range(span // half):
        rows = slice(g * half, (g + 1) * half)
        own_rows = slice(first + g * half, first + (g + 1) * half)
        partner = jnp.concatenate([po_ref[own_rows, :], pr_ref[rows, :]], 0)
        resp = dot(mixed_ref[...], partner).astype(BF16)
        resp_ref[rows, :] = resp[:half]
        resp_ref[span + g * half : span + (g + 1) * half, :] = resp[half:]


def early_kernel(rows, so_ref, s_ref, resp_ref, *refs):
    out_ref = refs[-1]
    third = out_ref.shape[0] // 3
    for m in range(3):
        cols = slice(m * third, (m + 1) * third)
        both = jnp.concatenate([so_ref[rows, cols], s_ref[:, cols]], 0)
        part = dot_rows(both, resp_ref[...])
        for before_ref in refs[:-1]:
            part = part + before_ref[cols, :]
        out_ref[cols, :] = part


def terms_of(offsets, first, early_ref, so_ref, sr_ref, resp_ref, block):
    take = [slice((d + SPREAD) * block, (d + SPREAD + 1) * block) for d in offsets]
    rows = slice(first, first + sr_ref.shape[0])
    both = [jnp.concatenate([so_ref[rows, t], sr_ref[:, t]], 0) for t in take]
    total = dot_rows(jnp.concatenate(both, 1), resp_ref[...])
    return [total[n * block : (n + 1) * block] + early_ref[t, :] for n, t in enumerate(take)]


def placed_terms(ok, term, offset, first, count, block, dtype):
    tiles = []
    for c in range(first, first + count):
        source = c + offset
        if 0 <= source < SLOTS:
            tile = term[:, source * block : (source + 1) * block]
            tiles.append(jnp.where(ok, tile, jnp.zeros_like(tile)).astype(dtype))
        else:
            tiles.append(jnp.zeros((block, block), dtype))
    return tiles


def odd_kernel(
    nblocks, first, at_ref, prof_ref, mixed_ref, v_ref, s_ref, po_ref, so_ref, early_ref,
    pr_ref, resp_ref, pack_ref,
):
    respond_kernel(first, mixed_ref, v_ref, s_ref, po_ref, pr_ref, resp_ref)
    block = pack_ref.shape[1]
    position = at_ref[0]
    terms = terms_of(ODD, first, early_ref, so_ref, s_ref, resp_ref, block)
    for n, (offset, term) in enumerate(zip(ODD, terms)):
        ok = permitted(prof_ref, nblocks, position, position + offset)
        tiles = placed_terms(ok, term, offset, FIRST_COLUMN[offset], 8, block, BF16)
        for c, tile in enumerate(tiles):
            pack_ref[n, :, c * block : (c + 1) * block] = tile


def even_kernel(
    nblocks, first, at_ref, prof_ref, so_ref, s_ref, resp_ref, early_ref, own_ref, *out_refs
):
    block = own_ref.shape[0]
    position = at_ref[0]
    offsets = (0, 2, -2, 4, -4)
    terms = terms_of(offsets, first, early_ref, so_ref, s_ref, resp_ref, block)
    own_ref[...] = terms[0]
    for offset, term, out in zip(offsets[1:], terms[1:], out_refs):
        ok = permitted(prof_ref, nblocks, position, position + offset)
        begin, count = FIRST_COLUMN[offset], columns_to(offset)
        for c, tile in enumerate(placed_terms(ok, term, offset, begin, count, block, F32)):
            out[:, c * block : (c + 1) * block] = tile


def upward_first(position, distance):
    return lax.rem(position // distance, 2) == 0


def combine_kernel(at_ref, pack_ref, own_ref, u2_ref, d2_ref, u4_ref, d4_ref, *outs):
    mid_ref, first2_ref, second2_ref, first4_ref, second4_ref = outs
    block = own_ref.shape[0]
    ins = {0: own_ref, 2: u2_ref, -2: d2_ref, 4: u4_ref, -4: d4_ref}
    position = at_ref[0]
    odd = lax.rem(position, 2) == 1

    def merge(sources):
        def tile_of(offset, c):
            first = 0 if offset == 0 else FIRST_COLUMN[offset]
            value = ins[offset][:, c * block : (c + 1) * block]
            if offset in sources:
                n = sources[offset]
                at = c + first - FIRST_COLUMN[ODD[n]]
                if 0 <= at < 8:
                    value = value + pack_ref[n, :, at * block : (at + 1) * block].astype(F32)
            return value

        for c in range(SLOTS):
            mid_ref[:, c * block : (c + 1) * block] = tile_of(0, c)
        for distance, out1, out2 in ((2, first2_ref, second2_ref), (4, first4_ref, second4_ref)):
            upward = upward_first(position, distance)
            for c in range(out1.shape[1] // block):
                columns = slice(c * block, (c + 1) * block)
                up = tile_of(distance, c)
                down = tile_of(-distance, c)
                out1[:, columns] = jnp.where(upward, up, down).astype(BF16)
                out2[:, columns] = jnp.where(upward, down, up).astype(BF16)

    @pl.when(jnp.logical_not(odd))
    def _():
        merge({-2: 0, 0: 1, 2: 2, 4: 3})

    @pl.when(odd)
    def _():
        merge({-4: 0, -2: 1, 0: 2, 2: 3})


def gather_kernel(at_ref, own_ref, *refs):
    pieces, (keep_ref, send_ref) = {2: refs[:2], 4: refs[2:4]}, refs[4:]
    block = own_ref.shape[0]
    rows = keep_ref.shape[0]
    position, half = at_ref[0], at_ref[1]
    for target, which in ((send_ref, 1 - half), (keep_ref, half)):
        window = pl.ds(pl.multiple_of(which * rows, rows), rows)
        for c in range(SLOTS):
            columns = slice(c * block, (c + 1) * block)
            total = own_ref[window, columns]
            for distance, (one, two) in pieces.items():
                upward = upward_first(position, distance)
                for offset, above, below in ((distance, two, one), (-distance, one, two)):
                    at = c - FIRST_COLUMN[offset]
                    if 0 <= at < columns_to(offset):
                        tile = slice(at * block, (at + 1) * block)
                        part = jnp.where(upward, above[window, tile], below[window, tile])
                        total = total + part.astype(F32)
            target[:, columns] = total.astype(target.dtype)


def finish_kernel(
    nblocks, block, scale, polar_scale, at_ref, prof_ref, keep_ref, got_ref, pk_ref, pg_ref,
    out_ref, polar_ref,
):
    polar_ref[...] = (pk_ref[...] + pg_ref[...]) * polar_scale
    position = at_ref[0]
    for c in range(SLOTS):
        columns = slice(c * block, (c + 1) * block)
        ok = permitted(prof_ref, nblocks, position, position + c - SPREAD)
        value = (keep_ref[:, columns] + got_ref[:, columns].astype(F32)) * scale
        out_ref[:, columns] = jnp.where(ok, value, jnp.zeros_like(value))


def gram_of(size, x_ref, co_ref, po_ref, chunks, total):
    half = size // 2
    for first, s_ref, pr_ref in chunks:
        got = dot(s_ref[...], x_ref[...]).astype(BF16)
        for g in range(s_ref.shape[0] // half):
            rows = slice(g * half, (g + 1) * half)
            own_rows = slice(first + g * half, first + (g + 1) * half)
            coupled = jnp.concatenate([co_ref[own_rows, :], got[rows]], 0)
            partner = jnp.concatenate([po_ref[own_rows, :], pr_ref[rows, :]], 0)
            part = dot_columns(coupled, partner)
            total = part if total is None else total + part
    return total


def chunk_refs(firsts, refs):
    return list(zip(firsts, refs[::2], refs[1::2]))


def gram_kernel(firsts, x_ref, co_ref, po_ref, *refs):
    out_ref = refs[-1]
    chunks = chunk_refs(firsts, refs[:-1])
    out_ref[...] = gram_of(out_ref.shape[0], x_ref, co_ref, po_ref, chunks, None)


def polar_kernel(firsts, at_ref, x_ref, co_ref, po_ref, gram_ref, mine_ref, theirs_ref, *refs):
    out_ref = refs[-1]
    size = gram_ref.shape[0]
    every = out_ref.shape[0]
    here = every // 2
    chunks = chunk_refs(firsts, refs[:-1])
    total = gram_of(size, x_ref, co_ref, po_ref, chunks, gram_ref[...])
    by_row = jnp.sum(jnp.where(same_row(size), total, 0.0).reshape(every, SUB, size), 1)
    polar = jnp.dot(
        by_row, one_hot(size, every), preferred_element_type=F32, precision=lax.Precision.HIGHEST
    )
    row, alive = screen_row(mine_ref, theirs_ref)
    polar = polar * row * alive
    turned = jnp.concatenate([polar[:, here:], polar[:, :here]], 1)
    out_ref[...] = jnp.where(at_ref[1] == 0, polar, turned)


def step(occupied, virtual, three_centre, kernel, profile, atom_map):
    block, width = occupied.shape
    nblocks = lax.axis_size("chain")
    halves = lax.axis_size("aux")
    if halves != 2 or width != SLOTS * block or nblocks % 2:
        raise ValueError("unsupported mesh")
    position = lax.axis_index("chain")
    half = lax.axis_index("aux")
    here = three_centre.shape[0]
    every = kernel.shape[1]
    rows = block // halves
    groups = rows // SUB
    per_group = here * SUB
    most = -(-groups // 3)
    sizes = (most, most, groups - 2 * most)
    begins = (0, most, 2 * most)
    firsts = [g * per_group for g in begins]
    counts = [g * per_group for g in sizes]
    at = jnp.stack([position, half]).astype(jnp.int32)

    integrals = pltpu.with_memory_space_constraint(three_centre, pltpu.HBM)

    def cut(picks):
        lengths = [count for _, _, count in picks]
        call = pl.pallas_call(
            functools.partial(cut_kernel, rows, [pick[:2] for pick in picks]),
            out_shape=[shaped((count, here, SUB, width)) for count in lengths],
            in_specs=[SMEM, pl.BlockSpec(memory_space=pltpu.HBM)],
            out_specs=[VMEM] * len(picks),
            scratch_shapes=[pltpu.SemaphoreType.DMA((sum(lengths),))],
            compiler_params=pltpu.CompilerParams(vmem_limit_bytes=24 * 1024 * 1024),
            cost_estimate=pl.CostEstimate(
                flops=0, bytes_accessed=4 * sum(lengths) * per_group * width, transcendentals=0
            ),
        )
        parts = call(at, integrals)
        return [part.reshape(-1, width) for part in parts]

    def halo(band):
        mid = swapped(band, "chain")
        packs = run(
            pair_kernel,
            [at, band, mid],
            [shaped((block, 15 * block)), shaped((block, 11 * block))],
            smem=1,
        )
        hops = []
        for distance, pack in zip((2, 4), packs):
            up = [(i, i + distance) for i in range(0, nblocks - distance, 2)]
            down = [(i + distance, i) for i in range(1, nblocks - distance, 2)]
            hops.append(lax.ppermute(pack, "chain", up + down))
        return [band, mid, *hops, *[swapped(h, "chain") for h in hops]]

    sends = cut([(False, begins[0], sizes[0])])
    rest = [(False, f, n) for f, n in zip(begins[1:], sizes[1:])]
    *others, own = cut(rest + [(True, 0, groups)])
    got = [swapped(part, "aux") for part in [*sends, *others]]
    near_vir = halo(virtual)
    near_occ = halo(occupied)

    mine, send = run(
        functools.partial(prepare_kernel, nblocks),
        [at, atom_map, kernel],
        [shaped((here, 2 * every), F32)] * 2,
        smem=2,
    )
    theirs = swapped(send, "aux")

    (mixed,) = run(mixing_kernel, [mine, theirs], [shaped((every * SUB, every * SUB))])

    per_row = 2 * width * width
    own_flops = own.shape[0] * per_row

    def contracted(near):
        return run(
            functools.partial(stack_kernel, nblocks),
            [at, profile, *near, own],
            [shaped((width, width)), shaped(own.shape)],
            flops=own_flops,
            smem=2,
        )

    vir_stack, partner_own = contracted(near_vir)
    partner_got, responses = [], []
    for c in range(2):
        pr, resp = run(
            functools.partial(respond_kernel, firsts[c]),
            [mixed, vir_stack, got[c], partner_own],
            [shaped((counts[c], width)), shaped((2 * counts[c], width))],
            flops=2 * counts[c] * per_row,
        )
        partner_got.append(pr)
        responses.append(resp)
    early = []
    for c in range(2):
        early = run(
            functools.partial(early_kernel, slice(firsts[c], firsts[c] + counts[c])),
            [own, got[c], responses[c], *early],
            [shaped((width, width), F32)],
            flops=2 * counts[c] * per_row,
        )
    (early,) = early
    pr, resp, pack = run(
        functools.partial(odd_kernel, nblocks, firsts[2]),
        [at, profile, mixed, vir_stack, got[2], partner_own, own, early],
        [
            shaped((counts[2], width)),
            shaped((2 * counts[2], width)),
            shaped((len(ODD), block, 8 * block)),
        ],
        flops=2 * counts[2] * per_row,
        smem=2,
    )
    partner_got.append(pr)
    other_pack = swapped(pack, "chain")
    offsets = (2, -2, 4, -4)
    even = run(
        functools.partial(even_kernel, nblocks, firsts[2]),
        [at, profile, own, got[2], resp, early],
        [shaped((block, width), F32)]
        + [shaped((block, columns_to(d) * block), F32) for d in offsets],
        flops=counts[2] * per_row,
        smem=2,
    )
    mid, *sends = run(
        combine_kernel,
        [at, other_pack, *even],
        [shaped((block, width), F32)] + [shaped((block, columns_to(d) * block)) for d in offsets],
        smem=1,
    )
    arrived = []
    for n, send in enumerate(sends):
        distance, parity = (2, 2, 4, 4)[n], n % 2
        lower = [i for i in range(nblocks - distance) if i // distance % 2 == parity]
        route = [pair for i in lower for pair in ((i, i + distance), (i + distance, i))]
        arrived.append(lax.ppermute(send, "chain", route))
    keep, send = run(
        gather_kernel,
        [at, mid, *arrived],
        [shaped((rows, width), F32), shaped((rows, width))],
        smem=1,
    )
    occ_stack, coupled_own = contracted(near_occ)
    size = every * SUB
    (gram,) = run(
        functools.partial(gram_kernel, firsts[:2]),
        [occ_stack, coupled_own, partner_own, got[0], partner_got[0], got[1], partner_got[1]],
        [shaped((size, size), F32)],
        flops=firsts[2] * per_row,
    )
    (polar,) = run(
        functools.partial(polar_kernel, firsts[2:]),
        [at, occ_stack, coupled_own, partner_own, gram, mine, theirs, got[2], partner_got[2]],
        [shaped((every, every), F32)],
        flops=counts[2] * per_row,
        smem=1,
    )
    bits = [1 << n for n in range(nblocks.bit_length() - 1)]
    first = bits.pop(min(2, len(bits) - 1))
    polar = polar + swapped(polar, "chain", first)
    polar = polar[:here] + swapped(polar[here:], "aux")
    for n, bit in enumerate(bits):
        other = swapped(polar, "chain", bit)
        if n < len(bits) - 1:
            polar = polar + other
    return run(
        functools.partial(
            finish_kernel,
            nblocks,
            block,
            1.0 / math.sqrt(block * every),
            1.0 / math.sqrt(block * nblocks * width),
        ),
        [at, profile, keep, swapped(send, "aux"), polar, other],
        [shaped((rows, width), F32), shaped((here, every), F32)],
        smem=2,
    )


def solution(mesh):
    placed = (
        P("chain", None),
        P("chain", None),
        P("aux", "chain", None),
        P("aux", None),
        P(),
        P("aux"),
    )
    return jax.shard_map(
        step,
        mesh=mesh,
        in_specs=placed,
        out_specs=(P(("chain", "aux"), None), P("aux", None)),
        check_vma=False,
    )
```

```python
import functools
import math

import jax
import jax.numpy as jnp
from jax import lax
from jax.experimental import pallas as pl
from jax.experimental.pallas import tpu as pltpu
from jax.sharding import PartitionSpec as P


F32 = jnp.float32
BF16 = jnp.bfloat16
SUB = 8
SPREAD = 4
SLOTS = 9
VMEM = pl.BlockSpec(memory_space=pltpu.VMEM)
SMEM = pl.BlockSpec(memory_space=pltpu.SMEM)
FIRST_COLUMN = {2: 0, -2: 1, 4: 0, -4: 3, 1: 0, 3: 0, -1: 1, -3: 1}
ODD = (-3, -1, 1, 3)


def columns_to(offset):
    return 6 if abs(offset) == 4 else 8


def swapped(block, axis, bit=1):
    return lax.ppermute(block, axis, [(i, i ^ bit) for i in range(lax.axis_size(axis))])


def permitted(prof_ref, nblocks, a, b):
    last = nblocks - 1
    inside = (a >= 0) & (a <= last) & (b >= 0) & (b <= last)
    wide_a = prof_ref[jnp.clip(a, 0, last)]
    wide_b = prof_ref[jnp.clip(b, 0, last)]
    return inside & (jnp.abs(a - b) <= jnp.minimum(wide_a, wide_b))


def run(kernel, operands, outs, flops=0, smem=0, grant=24):
    nbytes = sum(math.prod(s.shape) * s.dtype.itemsize for s in (*operands, *outs))
    return pl.pallas_call(
        kernel,
        out_shape=outs,
        in_specs=[SMEM] * smem + [VMEM] * (len(operands) - smem),
        out_specs=[VMEM] * len(outs),
        compiler_params=pltpu.CompilerParams(vmem_limit_bytes=grant * 1024 * 1024),
        cost_estimate=pl.CostEstimate(
            flops=int(flops), bytes_accessed=int(nbytes), transcendentals=0
        ),
    )(*operands)


def shaped(shape, dtype=BF16):
    return jax.ShapeDtypeStruct(shape, dtype)


def dot(a, b):
    return jnp.dot(a, b, preferred_element_type=F32)


def dot_rows(a, b):
    return lax.dot_general(a, b, (((0,), (0,)), ((), ())), preferred_element_type=F32)


def dot_columns(a, b):
    return lax.dot_general(a, b, (((1,), (1,)), ((), ())), preferred_element_type=F32)


def prepare_kernel(nblocks, at_ref, atom_ref, k_ref, keep_ref, send_ref):
    here, every = k_ref.shape
    position, half = at_ref[0], at_ref[1]
    rows = lax.broadcasted_iota(jnp.int32, (here, every), 0)
    alive = jnp.zeros((here, every), F32)
    for p in range(here):
        near = jnp.abs(atom_ref[p] - position) <= nblocks // 4
        alive = jnp.where((rows == p) & near, 1.0, alive)
    plain = k_ref[...].astype(F32) * alive
    turned = jnp.concatenate([plain[:, here:], plain[:, :here]], 1)
    keep_ref[:, :every] = jnp.where(half == 0, plain, turned)
    keep_ref[:, every:] = alive
    send_ref[:, :every] = jnp.where(half == 0, turned, plain)
    send_ref[:, every:] = alive


def screen_row(mine_ref, theirs_ref):
    every = mine_ref.shape[1] // 2
    alive = jnp.concatenate([mine_ref[:, every:], theirs_ref[:, every:]], 0)
    r = lax.broadcasted_iota(jnp.int32, (every, every), 0)
    c = lax.broadcasted_iota(jnp.int32, (every, every), 1)
    return jnp.sum(jnp.where(r == c, alive, 0.0), 0, keepdims=True), alive


def one_hot(rows, cols):
    r = lax.broadcasted_iota(jnp.int32, (rows, cols), 0)
    c = lax.broadcasted_iota(jnp.int32, (rows, cols), 1)
    return (r // SUB == c).astype(F32)


def same_row(size):
    r = lax.broadcasted_iota(jnp.int32, (size, size), 0)
    c = lax.broadcasted_iota(jnp.int32, (size, size), 1)
    return lax.rem(r, SUB) == lax.rem(c, SUB)


def mixing_kernel(mine_ref, theirs_ref, out_ref):
    every = mine_ref.shape[1] // 2
    size = every * SUB
    row, _ = screen_row(mine_ref, theirs_ref)
    k = jnp.concatenate([mine_ref[:, :every], theirs_ref[:, :every]], 0) * row
    pick = one_hot(size, every).astype(BF16)
    wide = dot_columns(dot(pick, k.astype(BF16)).astype(BF16), pick)
    out_ref[...] = jnp.where(same_row(size), wide, 0.0).astype(BF16)


def band_slots(delta, which):
    sizes = {1: (7, 8), 2: (5, 6), -1: (8, 7), -2: (6, 5)}[delta]
    count = sizes[which]
    first = SLOTS - count if delta > 0 else 0
    return first, count, sizes[0] * which


def pair_kernel(at_ref, own_ref, mid_ref, out1_ref, out2_ref):
    block = own_ref.shape[0]

    def fill(sign, pair):
        for distance, out in ((1, out1_ref), (2, out2_ref)):
            for which in range(2):
                first, count, start = band_slots(sign * distance, which)
                out[:, start * block : (start + count) * block] = pair[which][
                    :, first * block : (first + count) * block
                ]

    odd = lax.rem(at_ref[0], 2) == 1

    @pl.when(jnp.logical_not(odd))
    def _():
        fill(1, (own_ref, mid_ref))

    @pl.when(odd)
    def _():
        fill(-1, (mid_ref, own_ref))


def stack_kernel(nblocks, at_ref, prof_ref, *refs):
    own_ref, mid_ref, hop1_ref, hop2_ref, near1_ref, near2_ref = refs[:6]
    rows_ref, stack_ref, out_ref = refs[6:]
    block = own_ref.shape[0]
    position = at_ref[0]

    def build(parity, pair, below, above):
        for offset in range(-SPREAD, SPREAD + 1):
            delta, which = divmod(parity + offset, 2)
            rows = slice((offset + SPREAD) * block, (offset + SPREAD + 1) * block)
            other = position + offset
            row_ok = permitted(prof_ref, nblocks, position, other)
            for col in range(SLOTS):
                slot = col - offset
                columns = slice(col * block, (col + 1) * block)
                if not 0 <= slot < SLOTS:
                    stack_ref[rows, columns] = jnp.zeros((block, block), BF16)
                    continue
                if delta == 0:
                    source, at = pair[which], slot
                else:
                    first, _, start = band_slots(-delta, which)
                    source = (below if delta < 0 else above)[abs(delta) - 1]
                    at = start + slot - first
                ok = row_ok & permitted(prof_ref, nblocks, other, position + col - SPREAD)
                tile = source[:, at * block : (at + 1) * block]
                stack_ref[rows, columns] = jnp.where(ok, tile, jnp.zeros_like(tile))

    odd = lax.rem(position, 2) == 1
    hops, nears = (hop1_ref, hop2_ref), (near1_ref, near2_ref)

    @pl.when(jnp.logical_not(odd))
    def _():
        build(0, (own_ref, mid_ref), hops, nears)

    @pl.when(odd)
    def _():
        build(1, (mid_ref, own_ref), nears, hops)

    part = out_ref.shape[0] // 4
    for n in range(4):
        rows = slice(n * part, (n + 1) * part)
        out_ref[rows, :] = dot(rows_ref[rows, :], stack_ref[...]).astype(BF16)


def cut_kernel(rows, picks, at_ref, three_ref, *refs):
    outs, sem = refs[:-1], refs[-1]
    copies = []
    for (mine, first), out in zip(picks, outs):
        which = at_ref[1] if mine else 1 - at_ref[1]
        for g in range(out.shape[0]):
            start = pl.multiple_of(which * rows + (first + g) * SUB, SUB)
            copies.append(
                pltpu.make_async_copy(
                    three_ref.at[:, pl.ds(start, SUB), :], out.at[g], sem.at[len(copies)]
                )
            )
    for copy in copies:
        copy.start()
    for copy in copies:
        copy.wait()


def respond_kernel(first, mixed_ref, v_ref, s_ref, po_ref, pr_ref, resp_ref):
    pr_ref[...] = dot(s_ref[...], v_ref[...]).astype(BF16)
    half = mixed_ref.shape[0] // 2
    span = s_ref.shape[0]
    for g in range(span // half):
        rows = slice(g * half, (g + 1) * half)
        own_rows = slice(first + g * half, first + (g + 1) * half)
        partner = jnp.concatenate([po_ref[own_rows, :], pr_ref[rows, :]], 0)
        resp = dot(mixed_ref[...], partner).astype(BF16)
        resp_ref[rows, :] = resp[:half]
        resp_ref[span + g * half : span + (g + 1) * half, :] = resp[half:]


def early_kernel(rows, so_ref, s_ref, resp_ref, *refs):
    out_ref = refs[-1]
    third = out_ref.shape[0] // 3
    for m in range(3):
        cols = slice(m * third, (m + 1) * third)
        both = jnp.concatenate([so_ref[rows, cols], s_ref[:, cols]], 0)
        part = dot_rows(both, resp_ref[...])
        for before_ref in refs[:-1]:
            part = part + before_ref[cols, :]
        out_ref[cols, :] = part


def terms_of(offsets, first, early_ref, so_ref, sr_ref, resp_ref, block):
    take = [slice((d + SPREAD) * block, (d + SPREAD + 1) * block) for d in offsets]
    rows = slice(first, first + sr_ref.shape[0])
    both = [jnp.concatenate([so_ref[rows, t], sr_ref[:, t]], 0) for t in take]
    total = dot_rows(jnp.concatenate(both, 1), resp_ref[...])
    return [total[n * block : (n + 1) * block] + early_ref[t, :] for n, t in enumerate(take)]


def placed_terms(ok, term, offset, first, count, block, dtype):
    tiles = []
    for c in range(first, first + count):
        source = c + offset
        if 0 <= source < SLOTS:
            tile = term[:, source * block : (source + 1) * block]
            tiles.append(jnp.where(ok, tile, jnp.zeros_like(tile)).astype(dtype))
        else:
            tiles.append(jnp.zeros((block, block), dtype))
    return tiles


def odd_kernel(
    nblocks, first, at_ref, prof_ref, mixed_ref, v_ref, s_ref, po_ref, so_ref, early_ref,
    pr_ref, resp_ref, pack_ref,
):
    respond_kernel(first, mixed_ref, v_ref, s_ref, po_ref, pr_ref, resp_ref)
    block = pack_ref.shape[1]
    position = at_ref[0]
    terms = terms_of(ODD, first, early_ref, so_ref, s_ref, resp_ref, block)
    for n, (offset, term) in enumerate(zip(ODD, terms)):
        ok = permitted(prof_ref, nblocks, position, position + offset)
        tiles = placed_terms(ok, term, offset, FIRST_COLUMN[offset], 8, block, BF16)
        for c, tile in enumerate(tiles):
            pack_ref[n, :, c * block : (c + 1) * block] = tile


def even_kernel(
    nblocks, first, at_ref, prof_ref, so_ref, s_ref, resp_ref, early_ref, own_ref, *out_refs
):
    block = own_ref.shape[0]
    position = at_ref[0]
    offsets = (0, 2, -2, 4, -4)
    terms = terms_of(offsets, first, early_ref, so_ref, s_ref, resp_ref, block)
    own_ref[...] = terms[0]
    for offset, term, out in zip(offsets[1:], terms[1:], out_refs):
        ok = permitted(prof_ref, nblocks, position, position + offset)
        begin, count = FIRST_COLUMN[offset], columns_to(offset)
        for c, tile in enumerate(placed_terms(ok, term, offset, begin, count, block, F32)):
            out[:, c * block : (c + 1) * block] = tile


def upward_first(position, distance):
    return lax.rem(position // distance, 2) == 0


def combine_kernel(at_ref, pack_ref, own_ref, u2_ref, d2_ref, u4_ref, d4_ref, *outs):
    mid_ref, first2_ref, second2_ref, first4_ref, second4_ref = outs
    block = own_ref.shape[0]
    ins = {0: own_ref, 2: u2_ref, -2: d2_ref, 4: u4_ref, -4: d4_ref}
    position = at_ref[0]
    odd = lax.rem(position, 2) == 1

    def merge(sources):
        def tile_of(offset, c):
            first = 0 if offset == 0 else FIRST_COLUMN[offset]
            value = ins[offset][:, c * block : (c + 1) * block]
            if offset in sources:
                n = sources[offset]
                at = c + first - FIRST_COLUMN[ODD[n]]
                if 0 <= at < 8:
                    value = value + pack_ref[n, :, at * block : (at + 1) * block].astype(F32)
            return value

        for c in range(SLOTS):
            mid_ref[:, c * block : (c + 1) * block] = tile_of(0, c)
        for distance, out1, out2 in ((2, first2_ref, second2_ref), (4, first4_ref, second4_ref)):
            upward = upward_first(position, distance)
            for c in range(out1.shape[1] // block):
                columns = slice(c * block, (c + 1) * block)
                up = tile_of(distance, c)
                down = tile_of(-distance, c)
                out1[:, columns] = jnp.where(upward, up, down).astype(BF16)
                out2[:, columns] = jnp.where(upward, down, up).astype(BF16)

    @pl.when(jnp.logical_not(odd))
    def _():
        merge({-2: 0, 0: 1, 2: 2, 4: 3})

    @pl.when(odd)
    def _():
        merge({-4: 0, -2: 1, 0: 2, 2: 3})


def gathered(position, which, c, own_ref, pieces):
    block = own_ref.shape[0]
    rows = block // 2
    window = pl.ds(pl.multiple_of(which * rows, rows), rows)
    total = own_ref[window, c * block : (c + 1) * block]
    for distance, one, two in ((2, *pieces[:2]), (4, *pieces[2:])):
        upward = upward_first(position, distance)
        for offset, above, below in ((distance, two, one), (-distance, one, two)):
            at = c - FIRST_COLUMN[offset]
            if 0 <= at < columns_to(offset):
                tile = slice(at * block, (at + 1) * block)
                part = jnp.where(upward, above[window, tile], below[window, tile])
                total = total + part.astype(F32)
    return total


def gather_kernel(at_ref, own_ref, *refs):
    block = own_ref.shape[0]
    send_ref = refs[4]
    for c in range(SLOTS):
        total = gathered(at_ref[0], 1 - at_ref[1], c, own_ref, refs[:4])
        send_ref[:, c * block : (c + 1) * block] = total.astype(BF16)


def finish_kernel(
    nblocks, block, scale, polar_scale, at_ref, prof_ref, own_ref, *refs
):
    *pieces, got_ref, pk_ref, pg_ref, out_ref, polar_ref = refs
    polar_ref[...] = (pk_ref[...] + pg_ref[...]) * polar_scale
    position = at_ref[0]
    for c in range(SLOTS):
        columns = slice(c * block, (c + 1) * block)
        ok = permitted(prof_ref, nblocks, position, position + c - SPREAD)
        kept = gathered(position, at_ref[1], c, own_ref, pieces)
        value = (kept + got_ref[:, columns].astype(F32)) * scale
        out_ref[:, columns] = jnp.where(ok, value, jnp.zeros_like(value))


def gram_of(size, x_ref, co_ref, po_ref, chunks, total):
    half = size // 2
    for first, s_ref, pr_ref in chunks:
        got = dot(s_ref[...], x_ref[...]).astype(BF16)
        for g in range(s_ref.shape[0] // half):
            rows = slice(g * half, (g + 1) * half)
            own_rows = slice(first + g * half, first + (g + 1) * half)
            coupled = jnp.concatenate([co_ref[own_rows, :], got[rows]], 0)
            partner = jnp.concatenate([po_ref[own_rows, :], pr_ref[rows, :]], 0)
            part = dot_columns(coupled, partner)
            total = part if total is None else total + part
    return total


def chunk_refs(firsts, refs):
    return list(zip(firsts, refs[::2], refs[1::2]))


def gram_kernel(firsts, x_ref, co_ref, po_ref, *refs):
    out_ref = refs[-1]
    chunks = chunk_refs(firsts, refs[:-1])
    out_ref[...] = gram_of(out_ref.shape[0], x_ref, co_ref, po_ref, chunks, None)


def polar_kernel(firsts, at_ref, x_ref, co_ref, po_ref, gram_ref, mine_ref, theirs_ref, *refs):
    out_ref = refs[-1]
    size = gram_ref.shape[0]
    every = out_ref.shape[0]
    here = every // 2
    chunks = chunk_refs(firsts, refs[:-1])
    total = gram_of(size, x_ref, co_ref, po_ref, chunks, gram_ref[...])
    by_row = jnp.sum(jnp.where(same_row(size), total, 0.0).reshape(every, SUB, size), 1)
    polar = jnp.dot(
        by_row, one_hot(size, every), preferred_element_type=F32, precision=lax.Precision.HIGHEST
    )
    row, alive = screen_row(mine_ref, theirs_ref)
    polar = polar * row * alive
    turned = jnp.concatenate([polar[:, here:], polar[:, :here]], 1)
    out_ref[...] = jnp.where(at_ref[1] == 0, polar, turned)


def step(occupied, virtual, three_centre, kernel, profile, atom_map):
    block, width = occupied.shape
    nblocks = lax.axis_size("chain")
    halves = lax.axis_size("aux")
    if halves != 2 or width != SLOTS * block or nblocks % 2:
        raise ValueError("unsupported mesh")
    position = lax.axis_index("chain")
    half = lax.axis_index("aux")
    here = three_centre.shape[0]
    every = kernel.shape[1]
    rows = block // halves
    groups = rows // SUB
    per_group = here * SUB
    most = -(-groups // 3)
    sizes = (most, most, groups - 2 * most)
    begins = (0, most, 2 * most)
    firsts = [g * per_group for g in begins]
    counts = [g * per_group for g in sizes]
    at = jnp.stack([position, half]).astype(jnp.int32)

    integrals = pltpu.with_memory_space_constraint(three_centre, pltpu.HBM)

    def cut(picks):
        lengths = [count for _, _, count in picks]
        call = pl.pallas_call(
            functools.partial(cut_kernel, rows, [pick[:2] for pick in picks]),
            out_shape=[shaped((count, here, SUB, width)) for count in lengths],
            in_specs=[SMEM, pl.BlockSpec(memory_space=pltpu.HBM)],
            out_specs=[VMEM] * len(picks),
            scratch_shapes=[pltpu.SemaphoreType.DMA((sum(lengths),))],
            compiler_params=pltpu.CompilerParams(vmem_limit_bytes=24 * 1024 * 1024),
            cost_estimate=pl.CostEstimate(
                flops=0, bytes_accessed=4 * sum(lengths) * per_group * width, transcendentals=0
            ),
        )
        parts = call(at, integrals)
        return [part.reshape(-1, width) for part in parts]

    def halo(band):
        mid = swapped(band, "chain")
        packs = run(
            pair_kernel,
            [at, band, mid],
            [shaped((block, 15 * block)), shaped((block, 11 * block))],
            smem=1,
        )
        hops = []
        for distance, pack in zip((2, 4), packs):
            up = [(i, i + distance) for i in range(0, nblocks - distance, 2)]
            down = [(i + distance, i) for i in range(1, nblocks - distance, 2)]
            hops.append(lax.ppermute(pack, "chain", up + down))
        return [band, mid, *hops, *[swapped(h, "chain") for h in hops]]

    sends = cut([(False, begins[0], sizes[0])])
    rest = [(False, f, n) for f, n in zip(begins[1:], sizes[1:])]
    *others, own = cut(rest + [(True, 0, groups)])
    got = [swapped(part, "aux") for part in [*sends, *others]]
    near_vir = halo(virtual)
    near_occ = halo(occupied)

    mine, send = run(
        functools.partial(prepare_kernel, nblocks),
        [at, atom_map, kernel],
        [shaped((here, 2 * every), F32)] * 2,
        smem=2,
    )
    theirs = swapped(send, "aux")

    (mixed,) = run(mixing_kernel, [mine, theirs], [shaped((every * SUB, every * SUB))])

    per_row = 2 * width * width
    own_flops = own.shape[0] * per_row

    def contracted(near):
        return run(
            functools.partial(stack_kernel, nblocks),
            [at, profile, *near, own],
            [shaped((width, width)), shaped(own.shape)],
            flops=own_flops,
            smem=2,
        )

    vir_stack, partner_own = contracted(near_vir)
    partner_got, responses = [], []
    for c in range(2):
        pr, resp = run(
            functools.partial(respond_kernel, firsts[c]),
            [mixed, vir_stack, got[c], partner_own],
            [shaped((counts[c], width)), shaped((2 * counts[c], width))],
            flops=2 * counts[c] * per_row,
        )
        partner_got.append(pr)
        responses.append(resp)
    early = []
    for c in range(2):
        early = run(
            functools.partial(early_kernel, slice(firsts[c], firsts[c] + counts[c])),
            [own, got[c], responses[c], *early],
            [shaped((width, width), F32)],
            flops=2 * counts[c] * per_row,
        )
    (early,) = early
    pr, resp, pack = run(
        functools.partial(odd_kernel, nblocks, firsts[2]),
        [at, profile, mixed, vir_stack, got[2], partner_own, own, early],
        [
            shaped((counts[2], width)),
            shaped((2 * counts[2], width)),
            shaped((len(ODD), block, 8 * block)),
        ],
        flops=2 * counts[2] * per_row,
        smem=2,
    )
    partner_got.append(pr)
    other_pack = swapped(pack, "chain")
    offsets = (2, -2, 4, -4)
    even = run(
        functools.partial(even_kernel, nblocks, firsts[2]),
        [at, profile, own, got[2], resp, early],
        [shaped((block, width), F32)]
        + [shaped((block, columns_to(d) * block), F32) for d in offsets],
        flops=counts[2] * per_row,
        smem=2,
    )
    mid, *sends = run(
        combine_kernel,
        [at, other_pack, *even],
        [shaped((block, width), F32)] + [shaped((block, columns_to(d) * block)) for d in offsets],
        smem=1,
    )
    arrived = []
    for n, send in enumerate(sends):
        distance, parity = (2, 2, 4, 4)[n], n % 2
        lower = [i for i in range(nblocks - distance) if i // distance % 2 == parity]
        route = [pair for i in lower for pair in ((i, i + distance), (i + distance, i))]
        arrived.append(lax.ppermute(send, "chain", route))
    (send,) = run(gather_kernel, [at, mid, *arrived], [shaped((rows, width))], smem=1)

    occ_stack, coupled_own = contracted(near_occ)
    size = every * SUB
    (gram,) = run(
        functools.partial(gram_kernel, firsts[:2]),
        [occ_stack, coupled_own, partner_own, got[0], partner_got[0], got[1], partner_got[1]],
        [shaped((size, size), F32)],
        flops=firsts[2] * per_row,
    )
    (polar,) = run(
        functools.partial(polar_kernel, firsts[2:]),
        [at, occ_stack, coupled_own, partner_own, gram, mine, theirs, got[2], partner_got[2]],
        [shaped((every, every), F32)],
        flops=counts[2] * per_row,
        smem=1,
    )
    bits = [1 << n for n in range(nblocks.bit_length() - 1)]
    first = bits.pop(min(2, len(bits) - 1))
    polar = polar + swapped(polar, "chain", first)
    polar = polar[:here] + swapped(polar[here:], "aux")
    for n, bit in enumerate(bits):
        other = swapped(polar, "chain", bit)
        if n < len(bits) - 1:
            polar = polar + other
    return run(
        functools.partial(
            finish_kernel,
            nblocks,
            block,
            1.0 / math.sqrt(block * every),
            1.0 / math.sqrt(block * nblocks * width),
        ),
        [at, profile, mid, *arrived, swapped(send, "aux"), polar, other],
        [shaped((rows, width), F32), shaped((here, every), F32)],
        smem=2,
    )


def solution(mesh):
    placed = (
        P("chain", None),
        P("chain", None),
        P("aux", "chain", None),
        P("aux", None),
        P(),
        P("aux"),
    )
    return jax.shard_map(
        step,
        mesh=mesh,
        in_specs=placed,
        out_specs=(P(("chain", "aux"), None), P("aux", None)),
        check_vma=False,
    )
```
